32 devices in a mesh: section: 2 (over core), dp: 8 (over z, x), rep: 2 (over y).
Axes of the slice: x: 2, y: 2, z: 4, core: 2. Of those that a mesh axis runs over, the one named last changes fastest.
Arguments:
- inputs: bfloat16 [4096, 1024], P(('dp', 'rep')), may hold values from -6 to 6
- cotangent: bfloat16 [4096, 1024], P(('dp', 'rep')), may hold values from -6 to 6
- seg_counts: int32 [256], P(('dp', 'rep')), may hold values from 2 to 16
- w_qkv: bfloat16 [2, 1024, 3072], P('section'), may hold values from -0.1875 to 0.1875
- w_out: bfloat16 [2, 1024, 1024], P('section'), may hold values from -0.375 to 0.375
- w_up: bfloat16 [2, 1024, 2048], P('section'), may hold values from -0.1875 to 0.1875
- w_down: bfloat16 [2, 2048, 1024], P('section'), may hold values from -0.1875 to 0.1875
- gains: float32 [2, 2, 1024], P('section'), may hold values from 0.5 to 1.5
- biases: float32 [2, 2, 1024], P('section'), may hold values from -3 to 3
Outputs:
- layer_outputs: bfloat16 [2, 4096, 1024], P('section', ('dp', 'rep'))
- input_grads: bfloat16 [2, 4096, 1024], P('section', ('dp', 'rep'))
- grad_qkv: float32 [2, 1024, 3072], P('section', 'dp')
- grad_wout: float32 [2, 1024, 1024], P('section', None, 'dp')
- grad_up: float32 [2, 1024, 2048], P('section', 'dp')
- grad_down: float32 [2, 2048, 1024], P('section', None, 'dp')
- grad_gains: float32 [2, 2, 1024], P('section', None, 'dp')
- grad_biases: float32 [2, 2, 1024], P('section', None, 'dp')
The draws below stay inside these ranges and needn't reach their ends.
Inputs may be any that keep to these rules, and one draw needn't show every extreme that they name: seg_counts gives each series' number of valid slots; the first 16 - seg_counts slots of a series are padding.
All inputs are finite; a program needn't handle non-finite values.
Results may differ from the reference program's by a relative error of at most 0.015.
Values may be sent and summed in bfloat16 or wider, within the bound.
A program may use at most 256 MiB of HBM per device.

```python
import math
import jax
import jax.numpy as jnp
from jax import lax

D = 1024
HEADS = 8
FF = 2048
SEG = 16
HEAD_DIM = 128
LAYERS = 2
SERIES = 256
TOKENS = 4096


def plant(entries, key, low, high):
    longest = entries.shape.index(max(entries.shape))
    spots = []
    for shift in (0, 1):
        where = [jax.random.randint(jax.random.fold_in(key, axis), (), 0, length) for axis, length in enumerate(entries.shape)]
        where[longest] = (where[longest] + shift) % entries.shape[longest]
        spots.append(tuple(where))
    return entries.at[spots[0]].set(low).at[spots[1]].set(high)


def with_spikes(array, stream_key, source, target, parts, factor):
    def block_of(dim):
        return (jnp.arange(array.shape[dim]) // (array.shape[dim] // parts)).reshape((-1,) + (1,) * (array.ndim - 1 - dim))

    near = jax.random.permutation(stream_key, parts)[block_of(target)]
    other_side = (block_of(target) + parts // 2) % parts
    return jnp.where((block_of(source) == near) | (block_of(source) == other_side), factor * array, array)


def block_scale(own_key, dims, split, smallest, top_value):
    def one(axis_at, blocks):
        steps = jax.random.uniform(jax.random.fold_in(jax.random.fold_in(own_key, 6), axis_at), (blocks,), jnp.float32, smallest / len(split), top_value / len(split))
        return jnp.repeat(jnp.exp(steps), dims[axis_at] // blocks).reshape((-1,) + (1,) * (len(dims) - axis_at - 1))

    gain = one(*split[0])
    for cut in split[1:]:
        gain = gain * one(*cut)
    return gain


def bell_draw(rng, extent, scale, limit, cuts=(), kind=jnp.bfloat16):
    array = scale * jax.random.normal(rng, extent, jnp.float32)
    if cuts:
        array = array * block_scale(rng, extent, cuts, -0.22, 0.18)
    return jnp.clip(array, -limit, limit).astype(kind)


def noise_with(rng, shape, deviation, bound, cuts, heavy, held_as=jnp.bfloat16):
    values = deviation * jax.random.normal(rng, shape, jnp.float32)
    if cuts:
        values = values * block_scale(rng, shape, cuts, -0.22, 0.18)
    return jnp.clip(with_spikes(values, jax.random.fold_in(rng, 3), *heavy), -bound, bound).astype(held_as)


def setup_inputs(seed: int = 0) -> dict:
    keys = jax.random.split(jax.random.key(seed), 10)
    inputs = noise_with(keys[0], (TOKENS, D), 1.0, 6.0, ((0, 16),), (0, 1, 16, 2.0))
    cotangent = bell_draw(keys[1], (TOKENS, D), 1.0, 6.0, ((0, 16),))
    seg_counts = plant(jax.random.randint(keys[2], (SERIES,), 2, SEG + 1), jax.random.fold_in(keys[2], 1), 2, SEG).astype(jnp.int32)
    w_qkv = bell_draw(keys[3], (LAYERS, D, 3 * D), D ** -0.5, 0.1875, ((0, 2),))
    w_out = bell_draw(keys[4], (LAYERS, D, D), (D // 4) ** -0.5, 0.375, ((0, 2),))
    w_up = bell_draw(keys[5], (LAYERS, D, FF), D ** -0.5, 0.1875, ((0, 2),))
    w_down = bell_draw(keys[6], (LAYERS, FF, D), (FF // 2) ** -0.5, 0.1875, ((0, 2),))
    gains = jnp.clip(0.5 + 1.0 * jax.random.uniform(keys[7], (LAYERS, 2, D), jnp.float32) ** block_scale(keys[7], (LAYERS, 2, D), ((0, 2),), -0.2, 0.2), 0.5, 1.5)
    biases = bell_draw(keys[8], (LAYERS, 2, D), 0.5, 3.0, ((0, 2),), jnp.float32)
    return {"inputs": inputs, "cotangent": cotangent, "seg_counts": seg_counts, "w_qkv": w_qkv, "w_out": w_out, "w_up": w_up, "w_down": w_down, "gains": gains, "biases": biases}


epsilon = 1e-05
highest = lax.Precision.HIGHEST

@jax.custom_vjp
def low(v):
    return lax.optimization_barrier(v.astype(jnp.bfloat16)).astype(jnp.float32)

@jax.custom_vjp
def low_back(v):
    return v

def low_keep(v):
    return (low(v), None)

def low_pass(kept, grad):
    return (grad,)

def back_keep(v):
    return (v, None)

def back_low(kept, grad):
    return (low(grad),)
low.defvjp(low_keep, low_pass)
low_back.defvjp(back_keep, back_low)

def normalize(hidden):
    average = lax.optimization_barrier(jnp.mean(hidden, axis=-1, keepdims=True))
    centred = hidden - average
    return centred * lax.rsqrt(lax.optimization_barrier(jnp.mean(centred * centred, axis=-1, keepdims=True)) + epsilon)

def series_mask(counts):
    position = jnp.arange(SEG, dtype=jnp.int32)
    first = (SEG - counts)[:, None, None]
    causal = position[None, None, :] <= position[None, :, None]
    valid = position[None, None, :] >= first
    same = position[None, None, :] == position[None, :, None]
    return causal & (valid | same)

def layer(hidden, params, counts):
    w_qkv, w_out, w_up, w_down, gains, biases = params
    number = counts.shape[0]
    rows = number * SEG
    first_in = low(normalize(hidden) * gains[0] + biases[0])
    packed = low(low_back(jnp.dot(first_in, w_qkv, precision=highest)))
    packed = packed.reshape(number, SEG, 3, HEADS, HEAD_DIM)
    scores = jnp.einsum('sqhd,skhd->shqk', packed[:, :, 0], packed[:, :, 1], precision=highest) * HEAD_DIM ** (-0.5)
    scores = low_back(scores)
    scores = jnp.where(series_mask(counts)[:, None], scores, -1e+30)
    largest = lax.optimization_barrier(jnp.max(scores, axis=-1, keepdims=True))
    raised = jnp.exp(scores - largest)
    probs = low(raised / lax.optimization_barrier(jnp.sum(raised, axis=-1, keepdims=True)))
    mixed = jnp.einsum('shqk,skhd->sqhd', probs, packed[:, :, 2], precision=highest).reshape(rows, HEADS * HEAD_DIM)
    mixed = low(low_back(mixed))
    middle = hidden + low_back(jnp.dot(mixed, w_out, precision=highest))
    second_in = low(normalize(middle) * gains[1] + biases[1])
    upper = low_back(jnp.dot(second_in, w_up, precision=highest))
    activated = low(jax.nn.gelu(upper, approximate=True))
    return low(low_back(middle + low_back(jnp.dot(activated, w_down, precision=highest))))

def reference(inputs, cotangent, seg_counts, w_qkv, w_out, w_up, w_down, gains, biases):
    stacked = tuple((weight.astype(jnp.float32) for weight in (w_qkv, w_out, w_up, w_down, gains, biases)))
    layers = w_qkv.shape[0]
    width = inputs.shape[1]
    block_series = math.gcd(SERIES, 256)
    blocks = SERIES // block_series
    rows = block_series * SEG
    feed = inputs.astype(jnp.float32).reshape(blocks, rows, width)
    returned = cotangent.astype(jnp.float32).reshape(blocks, rows, width)
    counts_all = seg_counts.reshape(blocks, block_series)

    def advance(totals, pieces):
        hidden, upstream, block_counts = pieces
        outputs = []
        backs = []
        for layer_id in range(layers):
            params = tuple((weight[layer_id] for weight in stacked))
            hidden, back = jax.vjp(lambda state, weights: layer(state, weights, block_counts), hidden, params)
            outputs.append(hidden)
            backs.append(back)
        grads_in = [None] * layers
        grads_w = [None] * layers
        for layer_id in reversed(range(layers)):
            upstream, grads_w[layer_id] = backs[layer_id](upstream)
            grads_in[layer_id] = upstream
        totals = tuple((total + jnp.stack([grads[member] for grads in grads_w]) for member, total in enumerate(totals)))
        return (totals, (jnp.stack(outputs).astype(jnp.bfloat16), jnp.stack(grads_in).astype(jnp.bfloat16)))
    start = tuple((jnp.zeros(weight.shape, jnp.float32) for weight in stacked))
    totals, (outputs, grads_in) = lax.scan(advance, start, (feed, returned, counts_all))
    layer_outputs = jnp.swapaxes(outputs, 0, 1).reshape(layers, blocks * rows, width)
    input_grads = jnp.swapaxes(grads_in, 0, 1).reshape(layers, blocks * rows, width)
    return (layer_outputs, input_grads, totals[0], totals[1], totals[2], totals[3], totals[4], totals[5])
```

```python
from functools import partial

import jax
import jax.numpy as jnp
from jax import lax
from jax.sharding import PartitionSpec as P

SEG = 16
HEAD_DIM = 128
BLOCK = 128
epsilon = 1e-05
f32 = jnp.float32
bf16 = jnp.bfloat16


def normalize(hidden):
    average = jnp.mean(hidden, axis=-1, keepdims=True)
    centred = hidden - average
    inverse = lax.rsqrt(jnp.mean(centred * centred, axis=-1, keepdims=True) + epsilon)
    return (centred * inverse, inverse)


def normalize_back(grad_normed, normed, inverse):
    centre_term = jnp.mean(grad_normed, axis=-1, keepdims=True)
    slope_term = normed * jnp.mean(grad_normed * normed, axis=-1, keepdims=True)
    return inverse * (grad_normed - centre_term - slope_term)


def allowed_pairs(counts):
    rows = counts.shape[0] * SEG
    blocks = rows // BLOCK
    ids = jnp.arange(rows, dtype=jnp.int32).reshape(blocks, BLOCK)
    first = jnp.repeat(SEG - counts, SEG).reshape(blocks, BLOCK)
    position = ids % SEG
    owner = ids // SEG
    same = owner[:, :, None] == owner[:, None, :]
    causal = position[:, None, :] <= position[:, :, None]
    valid = (position >= first)[:, None, :] | (ids[:, :, None] == ids[:, None, :])
    return same & causal & valid


def forward(hidden_b, params, allowed):
    w_qkv, w_out, w_up, w_down, gains, biases = params
    rows = hidden_b.shape[0]
    heads = w_qkv.shape[1] // (3 * HEAD_DIM)
    hidden = hidden_b.astype(f32)
    n1, i1 = normalize(hidden)
    a = (n1 * gains[0] + biases[0]).astype(bf16)
    packed = jnp.dot(a, w_qkv, preferred_element_type=f32).astype(bf16)
    split = packed.reshape(rows // BLOCK, BLOCK, 3, heads, HEAD_DIM)
    scores = jnp.einsum("bqhd,bkhd->bhqk", split[:, :, 0], split[:, :, 1], preferred_element_type=f32)
    scores = jnp.where(allowed[:, None], scores * HEAD_DIM**-0.5, -1e30)
    raised = jnp.exp(scores - jnp.max(scores, axis=-1, keepdims=True))
    probs = raised / jnp.sum(raised, axis=-1, keepdims=True)
    probs_b = probs.astype(bf16)
    mixed = jnp.einsum("bhqk,bkhd->bqhd", probs_b, split[:, :, 2], preferred_element_type=f32)
    mixed_b = mixed.reshape(rows, heads * HEAD_DIM).astype(bf16)
    middle = hidden + jnp.dot(mixed_b, w_out, preferred_element_type=f32)
    n2, i2 = normalize(middle)
    c = (n2 * gains[1] + biases[1]).astype(bf16)
    upper = jnp.dot(c, w_up, preferred_element_type=f32)
    g = jax.nn.gelu(upper, approximate=True).astype(bf16)
    result = (middle + jnp.dot(g, w_down, preferred_element_type=f32)).astype(bf16)
    return result, (n1, i1, a, split, probs, probs_b, mixed_b, n2, i2, c, upper, g)


def backward(saved, grad_b, params):
    w_qkv, w_out, w_up, w_down, gains, biases = params
    n1, i1, a, split, probs, probs_b, mixed_b, n2, i2, c, upper, g = saved
    rows = grad_b.shape[0]
    heads = w_qkv.shape[1] // (3 * HEAD_DIM)
    d_g = jnp.einsum("rd,fd->rf", grad_b, w_down, preferred_element_type=f32)
    d_u = jax.vjp(partial(jax.nn.gelu, approximate=True), upper)[1](d_g)[0].astype(bf16)
    d_c = jnp.einsum("rf,df->rd", d_u, w_up, preferred_element_type=f32)
    d_m = grad_b.astype(f32) + normalize_back(d_c * gains[1], n2, i2)
    d_mb = d_m.astype(bf16)
    d_o = jnp.einsum("ro,io->ri", d_mb, w_out, preferred_element_type=f32).astype(bf16)
    d_o = d_o.reshape(rows // BLOCK, BLOCK, heads, HEAD_DIM)
    d_probs = jnp.einsum("bqhd,bkhd->bhqk", d_o, split[:, :, 2], preferred_element_type=f32)
    d_v = jnp.einsum("bhqk,bqhd->bkhd", probs_b, d_o, preferred_element_type=f32)
    d_s = (probs * (d_probs - jnp.sum(probs * d_probs, axis=-1, keepdims=True))).astype(bf16)
    d_q = jnp.einsum("bhqk,bkhd->bqhd", d_s, split[:, :, 1], preferred_element_type=f32) * HEAD_DIM**-0.5
    d_k = jnp.einsum("bhqk,bqhd->bkhd", d_s, split[:, :, 0], preferred_element_type=f32) * HEAD_DIM**-0.5
    d_p = jnp.stack((d_q, d_k, d_v), axis=2).reshape(rows, -1).astype(bf16)
    d_a = jnp.einsum("re,de->rd", d_p, w_qkv, preferred_element_type=f32)
    d_h = (d_m + normalize_back(d_a * gains[0], n1, i1)).astype(bf16)
    return d_h, (d_u, d_mb, d_p, d_a, d_c)


def per_device(inputs, cotangent, seg_counts, w_qkv, w_out, w_up, w_down, gains, biases):
    last = lax.axis_size("section") - 1
    section = lax.axis_index("section")
    params = (w_qkv[0], w_out[0], w_up[0], w_down[0], gains[0], biases[0])
    allowed = allowed_pairs(seg_counts)
    sent = forward(inputs, params, allowed)[0]
    hidden = jnp.where(section == 0, inputs, lax.ppermute(sent, "section", [(0, 1)]))
    result, saved = forward(hidden, params, allowed)
    sent = backward(saved, cotangent, params)[0]
    grad = jnp.where(section == last, cotangent, lax.ppermute(sent, "section", [(1, 0)]))
    d_h, (d_u, d_mb, d_p, d_a, d_c) = backward(saved, grad, params)
    n1, i1, a, split, probs, probs_b, mixed_b, n2, i2, c, upper, g = saved

    def outer(left, right):
        return jnp.einsum("ri,ro->io", left, right, preferred_element_type=f32).astype(bf16)[None]

    terms = (outer(a, d_p), outer(mixed_b, d_mb), outer(c, d_u), outer(g, grad))
    small_g = jnp.stack((jnp.sum(d_a * n1, axis=0), jnp.sum(d_c * n2, axis=0)))[None]
    small_b = jnp.stack((jnp.sum(d_a, axis=0), jnp.sum(d_c, axis=0)))[None]
    terms = terms + (small_g, small_b)
    dims = (1, 2, 1, 2, 2, 2)
    shares = [
        lax.psum_scatter(term, "dp", scatter_dimension=dim, tiled=True) for term, dim in zip(terms, dims)
    ]
    summed = [lax.psum(share.astype(bf16), "rep").astype(f32) for share in shares]
    return (result[None], d_h[None], *summed)


def solution(mesh):
    rows = P(("dp", "rep"), None)
    layer = P("section", None, None)
    return jax.shard_map(
        per_device,
        mesh=mesh,
        in_specs=(rows, rows, P(("dp", "rep"))) + (layer,) * 6,
        out_specs=(
            P("section", ("dp", "rep"), None),
            P("section", ("dp", "rep"), None),
            P("section", "dp", None),
            P("section", None, "dp"),
            P("section", "dp", None),
            P("section", None, "dp"),
            P("section", None, "dp"),
            P("section", None, "dp"),
        ),
        check_vma=False,
    )
```

```python
from functools import partial

import jax
import jax.numpy as jnp
from jax import lax
from jax.experimental import pallas as pl
from jax.experimental.pallas import tpu as pltpu
from jax.sharding import PartitionSpec as P

SEG = 16
HEAD_DIM = 128
BLOCK = 128
epsilon = 1e-05
f32 = jnp.float32
bf16 = jnp.bfloat16


def normalize(hidden):
    average = jnp.mean(hidden, axis=-1, keepdims=True)
    centred = hidden - average
    inverse = lax.rsqrt(jnp.mean(centred * centred, axis=-1, keepdims=True) + epsilon)
    return (centred * inverse, inverse)


def normalize_back(grad_normed, normed, inverse):
    centre_term = jnp.mean(grad_normed, axis=-1, keepdims=True)
    slope_term = normed * jnp.mean(grad_normed * normed, axis=-1, keepdims=True)
    return inverse * (grad_normed - centre_term - slope_term)


def allowed_pairs(counts):
    rows = counts.shape[0] * SEG
    blocks = rows // BLOCK
    ids = jnp.arange(rows, dtype=jnp.int32).reshape(blocks, BLOCK)
    first = jnp.repeat(SEG - counts, SEG).reshape(blocks, BLOCK)
    position = ids % SEG
    owner = ids // SEG
    same = owner[:, :, None] == owner[:, None, :]
    causal = position[:, None, :] <= position[:, :, None]
    valid = (position >= first)[:, None, :] | (ids[:, :, None] == ids[:, None, :])
    return same & causal & valid


def forward(hidden_b, params, allowed):
    w_qkv, w_out, w_up, w_down, gains, biases = params
    rows = hidden_b.shape[0]
    heads = w_qkv.shape[1] // (3 * HEAD_DIM)
    hidden = hidden_b.astype(f32)
    n1, i1 = normalize(hidden)
    a = (n1 * gains[0] + biases[0]).astype(bf16)
    packed = jnp.dot(a, w_qkv, preferred_element_type=f32).astype(bf16)
    split = packed.reshape(rows // BLOCK, BLOCK, 3, heads, HEAD_DIM)
    scores = jnp.einsum("bqhd,bkhd->bhqk", split[:, :, 0], split[:, :, 1], preferred_element_type=f32)
    scores = jnp.where(allowed[:, None], scores * HEAD_DIM**-0.5, -1e30)
    raised = jnp.exp(scores - jnp.max(scores, axis=-1, keepdims=True))
    probs = raised / jnp.sum(raised, axis=-1, keepdims=True)
    probs_b = probs.astype(bf16)
    mixed = jnp.einsum("bhqk,bkhd->bqhd", probs_b, split[:, :, 2], preferred_element_type=f32)
    mixed_b = mixed.reshape(rows, heads * HEAD_DIM).astype(bf16)
    middle = hidden + jnp.dot(mixed_b, w_out, preferred_element_type=f32)
    n2, i2 = normalize(middle)
    c = (n2 * gains[1] + biases[1]).astype(bf16)
    upper = jnp.dot(c, w_up, preferred_element_type=f32)
    g = jax.nn.gelu(upper, approximate=True).astype(bf16)
    result = (middle + jnp.dot(g, w_down, preferred_element_type=f32)).astype(bf16)
    return result, (n1, i1, a, split, probs, probs_b, mixed_b, n2, i2, c, upper, g)


def backward(saved, grad_b, params):
    w_qkv, w_out, w_up, w_down, gains, biases = params
    n1, i1, a, split, probs, probs_b, mixed_b, n2, i2, c, upper, g = saved
    rows = grad_b.shape[0]
    heads = w_qkv.shape[1] // (3 * HEAD_DIM)
    d_g = jnp.einsum("rd,fd->rf", grad_b, w_down, preferred_element_type=f32)
    d_u = jax.vjp(partial(jax.nn.gelu, approximate=True), upper)[1](d_g)[0].astype(bf16)
    d_c = jnp.einsum("rf,df->rd", d_u, w_up, preferred_element_type=f32)
    d_m = grad_b.astype(f32) + normalize_back(d_c * gains[1], n2, i2)
    d_mb = d_m.astype(bf16)
    d_o = jnp.einsum("ro,io->ri", d_mb, w_out, preferred_element_type=f32).astype(bf16)
    d_o = d_o.reshape(rows // BLOCK, BLOCK, heads, HEAD_DIM)
    d_probs = jnp.einsum("bqhd,bkhd->bhqk", d_o, split[:, :, 2], preferred_element_type=f32)
    d_v = jnp.einsum("bhqk,bqhd->bkhd", probs_b, d_o, preferred_element_type=f32)
    d_s = (probs * (d_probs - jnp.sum(probs * d_probs, axis=-1, keepdims=True))).astype(bf16)
    d_q = jnp.einsum("bhqk,bkhd->bqhd", d_s, split[:, :, 1], preferred_element_type=f32) * HEAD_DIM**-0.5
    d_k = jnp.einsum("bhqk,bqhd->bkhd", d_s, split[:, :, 0], preferred_element_type=f32) * HEAD_DIM**-0.5
    d_p = jnp.stack((d_q, d_k, d_v), axis=2).reshape(rows, -1).astype(bf16)
    d_a = jnp.einsum("re,de->rd", d_p, w_qkv, preferred_element_type=f32)
    d_h = (d_m + normalize_back(d_a * gains[0], n1, i1)).astype(bf16)
    return d_h, (d_u, d_mb, d_p, d_a, d_c)


TILE = 512
TOK = 256
MESH = pl.DeviceIdType.MESH


def reduce_kernel(
    n1, n2, a_ref, dp_ref, o_ref, dm_ref, c_ref, du_ref, g_ref, e_ref, small_ref,
    out_ref, small_out,
    lt, ltr, rall, rr, xs, xr, zs, zr, own, ag, sx, sz, sy,
    y_send, y_recv, x_send, x_recv, z_send, z_recv, g_send, g_recv, s_send, s_recv,
):
    dp = n1 * n2
    width = lt.shape[1] * lt.shape[2]
    rows = width // dp
    tiles = rall.shape[1]
    sec = lax.axis_index("section")
    me = lax.axis_index("dp")
    rep = lax.axis_index("rep")
    hi, lo = me // n1, me % n1
    y_to = (sec, me, 1 - rep)

    def x_to(k):
        return (sec, hi * n1 + (lo + k) % n1, rep)

    def z_to(k):
        return (sec, ((hi + k) % n2) * n1 + lo, rep)

    barrier = pltpu.get_barrier_semaphore()
    peers = [y_to] + [x_to(k) for k in range(1, n1)] + [z_to(k) for k in range(1, n2)]
    for peer in peers:
        pl.semaphore_signal(barrier, inc=1, device_id=peer, device_id_type=MESH)
    pl.semaphore_wait(barrier, len(peers))

    for m, ref in enumerate((a_ref, dm_ref, c_ref, e_ref)):
        for b in range(width // 128):
            block = ref[:, b * 128 : (b + 1) * 128].T
            per = 128 // rows if rows < 128 else 1
            for q in range(per):
                j = b * per + q
                lt[m, j % n1, (j // n1) * rows : (j // n1 + 1) * rows, :] = block[q * rows : (q + 1) * rows]
    for t in range(dp_ref.shape[1] // TILE):
        rall[0, t] = dp_ref[:, t * TILE : (t + 1) * TILE]
    for t in range(o_ref.shape[1] // TILE):
        rall[0, dp_ref.shape[1] // TILE + t] = o_ref[:, t * TILE : (t + 1) * TILE]
    for t in range(du_ref.shape[1] // TILE):
        rall[1, t] = du_ref[:, t * TILE : (t + 1) * TILE]
    for t in range(g_ref.shape[1] // TILE):
        rall[1, du_ref.shape[1] // TILE + t] = g_ref[:, t * TILE : (t + 1) * TILE]
    split = jnp.where(rep == 0, dp_ref.shape[1] // TILE, du_ref.shape[1] // TILE)

    def remote(src, dst, ss, rs, to):
        return pltpu.make_async_remote_copy(
            src_ref=src, dst_ref=dst, send_sem=ss, recv_sem=rs, device_id=to, device_id_type=MESH
        )

    def y_lhs(h):
        return remote(lt.at[2 * (1 - rep) + h], ltr.at[h], y_send.at[tiles + h], y_recv.at[tiles + h], y_to)

    def y_tile(t):
        return remote(rall.at[1 - rep, t], rr.at[t], y_send.at[t], y_recv.at[t], y_to)

    def x_tile(k, t):
        return remote(xs.at[k - 1, t], xr.at[k - 1, t], x_send.at[k - 1, t], x_recv.at[k - 1, t], x_to(k))

    def z_tile(k, t):
        return remote(
            zs.at[t, (hi + k) % n2], zr.at[k - 1, t], z_send.at[k - 1, t], z_recv.at[k - 1, t], z_to(k)
        )

    def g_tile(t):
        return remote(ag.at[rep, t], ag.at[rep, t], g_send.at[t], g_recv.at[t], y_to)

    def small_x(k):
        return remote(small_ref.at[(lo + k) % n1], sx.at[k - 1], s_send.at[k - 1], s_recv.at[k - 1], x_to(k))

    def small_z(k):
        n = n1 - 1 + k - 1
        return remote(sz.at[0, (hi + k) % n2], sz.at[k, hi], s_send.at[n], s_recv.at[n], z_to(k))

    def small_y():
        n = n1 + n2 - 2
        return remote(sy.at[0], sy.at[1], s_send.at[n], s_recv.at[n], y_to)

    for k in range(1, n1):
        small_x(k).start()
    y_lhs(0).start()
    for t in range(4):
        y_tile(t).start()
    y_lhs(1).start()
    for t in range(4, tiles):
        y_tile(t).start()

    def product(t, which):
        h = jnp.where(t >= split, 1, 0)
        mine = jnp.dot(lt[2 * rep + h, which], rall[rep, t], preferred_element_type=f32)
        return mine + jnp.dot(ltr[h, which], rr[t], preferred_element_type=f32)

    def stage_a(t):
        @pl.when(t == 0)
        def _():
            y_lhs(0).wait_recv()

        @pl.when(t == 4)
        def _():
            y_lhs(1).wait_recv()

        y_tile(t).wait_recv()
        for k in range(1, n1):
            part = product(t, (lo + k) % n1).astype(bf16)
            for q in range(n2):
                xs[k - 1, t, q] = part[q * rows : (q + 1) * rows]
            x_tile(k, t).start()

    def stage_b(t):
        part = product(t, lo)
        for k in range(1, n1):
            x_tile(k, t).wait_recv()
        for q in range(n2):
            total = part[q * rows : (q + 1) * rows]
            for k in range(1, n1):
                total = total + xr[k - 1, t, q].astype(f32)
            zs[t, q] = total.astype(bf16)

            @pl.when(hi == q)
            def _():
                own[t] = total

        for k in range(1, n2):
            z_tile(k, t).start()

    def stage_c(t):
        total = own[t]
        for k in range(1, n2):
            z_tile(k, t).wait_recv()
            total = total + zr[k - 1, t].astype(f32)
        ag[rep, t] = total.astype(bf16)
        g_tile(t).start()

    def body(s, carry):
        for lag, stage in ((0, stage_a), (2, stage_b), (4, stage_c)):

            @pl.when((s >= lag) & (s < tiles + lag))
            def _():
                stage(s - lag)

        return carry

    lax.fori_loop(0, tiles + 4, body, 0)

    total = small_ref[lo]
    for k in range(1, n1):
        small_x(k).wait_recv()
        total = total + sx[k - 1]
    sz[0] = total
    for k in range(1, n2):
        small_z(k).start()
    total = sz[0, hi]
    for k in range(1, n2):
        small_z(k).wait_recv()
        total = total + sz[k, (hi - k + n2) % n2]
    sy[0] = total
    small_y().start()
    small_y().wait_recv()
    small_out[...] = sy[0] + sy[1]

    def drain(t, carry):
        remote(ag.at[1 - rep, t], ag.at[1 - rep, t], g_send.at[t], g_recv.at[t], y_to).wait_recv()
        out_ref[0, t] = ag[0, t]
        out_ref[1, t] = ag[1, t]
        y_tile(t).wait_send()
        for k in range(1, n1):
            x_tile(k, t).wait_send()
        for k in range(1, n2):
            z_tile(k, t).wait_send()
        g_tile(t).wait_send()
        return carry

    lax.fori_loop(0, tiles, drain, 0)
    for h in range(2):
        y_lhs(h).wait_send()
    for k in range(1, n1):
        small_x(k).wait_send()
    for k in range(1, n2):
        small_z(k).wait_send()
    small_y().wait_send()


def reduce_grads(a, d_p, o, d_m, c, d_u, g, e, small):
    dp = lax.axis_size("dp")
    n1 = 2 if dp < 16 else 4
    n2 = dp // n1
    width = a.shape[1]
    rows = width // dp
    tiles = (d_p.shape[1] + o.shape[1]) // TILE
    padded = jnp.concatenate((small, jnp.zeros_like(small))).reshape(8, n2, n1, rows)
    padded = jnp.transpose(padded, (2, 1, 0, 3))
    dma = pltpu.SemaphoreType.DMA
    vm = pltpu.VMEM
    scratch = [
        vm((4, n1, n2 * rows, TOK), bf16),
        vm((2, n1, n2 * rows, TOK), bf16),
        vm((2, tiles, TOK, TILE), bf16),
        vm((tiles, TOK, TILE), bf16),
        vm((n1 - 1, tiles, n2, rows, TILE), bf16),
        vm((n1 - 1, tiles, n2, rows, TILE), bf16),
        vm((tiles, n2, rows, TILE), bf16),
        vm((n2 - 1, tiles, rows, TILE), bf16),
        vm((tiles, rows, TILE), f32),
        vm((2, tiles, rows, TILE), bf16),
        vm((n1 - 1, n2, 8, rows), f32),
        vm((n2, n2, 8, rows), f32),
        vm((2, 8, rows), f32),
        dma((tiles + 2,)), dma((tiles + 2,)),
        dma((n1 - 1, tiles)), dma((n1 - 1, tiles)),
        dma((n2 - 1, tiles)), dma((n2 - 1, tiles)),
        dma((tiles,)), dma((tiles,)),
        dma((n1 + n2 - 1,)), dma((n1 + n2 - 1,)),
    ]
    vspec = pl.BlockSpec(memory_space=pltpu.VMEM)
    out, small_out = pl.pallas_call(
        partial(reduce_kernel, n1, n2),
        out_shape=(
            jax.ShapeDtypeStruct((2, tiles, rows, TILE), bf16),
            jax.ShapeDtypeStruct((8, rows), f32),
        ),
        in_specs=[vspec] * 9,
        out_specs=(vspec, vspec),
        scratch_shapes=scratch,
        name="reduce_grads",
        compiler_params=pltpu.CompilerParams(
            collective_id=0, has_side_effects=True, vmem_limit_bytes=60 * 1024 * 1024
        ),
    )(a, d_p, o, d_m, c, d_u, g, e, padded)
    attn = jnp.swapaxes(out[0], 0, 1).reshape(rows, -1).astype(f32)
    feed = jnp.swapaxes(out[1], 0, 1).reshape(rows, -1).astype(f32)
    return (
        attn[None, :, : d_p.shape[1]],
        attn[:, d_p.shape[1] :].T[None],
        feed[None, :, : d_u.shape[1]],
        feed[:, d_u.shape[1] :].T[None],
        small_out[None, 0:2],
        small_out[None, 2:4],
    )


def per_device(inputs, cotangent, seg_counts, w_qkv, w_out, w_up, w_down, gains, biases):
    last = lax.axis_size("section") - 1
    section = lax.axis_index("section")
    params = (w_qkv[0], w_out[0], w_up[0], w_down[0], gains[0], biases[0])
    allowed = allowed_pairs(seg_counts)
    sent = forward(inputs, params, allowed)[0]
    hidden = jnp.where(section == 0, inputs, lax.ppermute(sent, "section", [(0, 1)]))
    result, saved = forward(hidden, params, allowed)
    sent = backward(saved, cotangent, params)[0]
    grad = jnp.where(section == last, cotangent, lax.ppermute(sent, "section", [(1, 0)]))
    d_h, (d_u, d_mb, d_p, d_a, d_c) = backward(saved, grad, params)
    n1, i1, a, split, probs, probs_b, mixed_b, n2, i2, c, upper, g = saved

    small = jnp.stack(
        (jnp.sum(d_a * n1, axis=0), jnp.sum(d_c * n2, axis=0), jnp.sum(d_a, axis=0), jnp.sum(d_c, axis=0))
    )
    summed = reduce_grads(a, d_p, mixed_b, d_mb, c, d_u, g, grad, small)
    return (result[None], d_h[None], *summed)


def solution(mesh):
    rows = P(("dp", "rep"), None)
    layer = P("section", None, None)
    return jax.shard_map(
        per_device,
        mesh=mesh,
        in_specs=(rows, rows, P(("dp", "rep"))) + (layer,) * 6,
        out_specs=(
            P("section", ("dp", "rep"), None),
            P("section", ("dp", "rep"), None),
            P("section", "dp", None),
            P("section", None, "dp"),
            P("section", "dp", None),
            P("section", None, "dp"),
            P("section", None, "dp"),
            P("section", None, "dp"),
        ),
        check_vma=False,
    )
```

```python
from functools import partial

import jax
import jax.numpy as jnp
from jax import lax
from jax.experimental import pallas as pl
from jax.experimental.pallas import tpu as pltpu
from jax.sharding import PartitionSpec as P

SEG = 16
HEAD = 128
BLOCK = 128
TILE = 512
MESH = pl.DeviceIdType.MESH
epsilon = 1e-05
f32 = jnp.float32
bf16 = jnp.bfloat16
NN = (((1,), (0,)), ((), ()))
NT = (((1,), (1,)), ((), ()))
TN = (((0,), (0,)), ((), ()))


def mul(left, right, dims=NN):
    return lax.dot_general(left, right, dims, preferred_element_type=f32)


def normalize(hidden):
    average = jnp.mean(hidden, axis=-1, keepdims=True)
    centred = hidden - average
    inverse = lax.rsqrt(jnp.mean(centred * centred, axis=-1, keepdims=True) + epsilon)
    return (centred * inverse, inverse)


def normalize_back(grad_normed, normed, inverse):
    centre_term = jnp.mean(grad_normed, axis=-1, keepdims=True)
    slope_term = normed * jnp.mean(grad_normed * normed, axis=-1, keepdims=True)
    return inverse * (grad_normed - centre_term - slope_term)


def gelu_pair(u):
    k = 0.7978845608
    square = u * u
    t = jnp.tanh(k * (u + 0.044715 * u * square))
    half = 0.5 * (1.0 + t)
    slope = half + 0.5 * u * (1.0 - t * t) * (k * (1.0 + 3 * 0.044715 * square))
    return u * half, slope


def step_kernel(
    n1, n2, x_ref, ct_ref, count_ref, wq_hbm, wo_hbm, wu_hbm, wd_hbm, gain_ref, bias_ref,
    out_ref, dh_ref, gq_ref, go_ref, gu_ref, gd_ref, small_ref,
    wq, wo, wu, wd, hb, eb, norm1, norm2, inv1, inv2, ab, pb, cb, dmb, dob, probs, mm, gp, dcb, acc, mask,
    lt, ltr, ra, rr, xs, xr, zs, zr, own, ag, sx, sz, sy,
    w_sem, y_send, y_recv, x_send, x_recv, z_send, z_recv, g_send, g_recv, s_send, s_recv, p_send, p_recv,
):
    dp = n1 * n2
    rows, width = hb.shape
    blocks = rows // BLOCK
    heads = width // HEAD
    ff = wu.shape[1]
    shard = width // dp
    tiles = ra.shape[0] // 2
    scale = HEAD**-0.5
    sec = lax.axis_index("section")
    me = lax.axis_index("dp")
    rep = lax.axis_index("rep")
    hi, lo = me // n1, me % n1
    other = 1 - rep
    y_to = (sec, me, other)
    s_to = (1 - sec, me, rep)

    def x_to(k):
        return (sec, hi * n1 + (lo + k) % n1, rep)

    def z_to(k):
        return (sec, ((hi + k) % n2) * n1 + lo, rep)

    weights = [
        pltpu.make_async_copy(src.at[0], dst, w_sem.at[i])
        for i, (src, dst) in enumerate(((wq_hbm, wq), (wo_hbm, wo), (wu_hbm, wu), (wd_hbm, wd)))
    ]
    for copy in weights:
        copy.start()

    barrier = pltpu.get_barrier_semaphore()
    peers = [s_to, y_to] + [x_to(k) for k in range(1, n1)] + [z_to(k) for k in range(1, n2)]
    for peer in peers:
        pl.semaphore_signal(barrier, inc=1, device_id=peer, device_id_type=MESH)
    pl.semaphore_wait(barrier, len(peers))

    q_tiles, o_tiles, u_tiles = 3 * width // TILE, width // TILE, ff // TILE
    O_AT, U_AT, G_AT = q_tiles, tiles, tiles + u_tiles

    def early(r):
        return jnp.where(r == 0, o_tiles, u_tiles)

    def rhs_of(r, t):
        return r * tiles + (t + tiles - early(r)) % tiles

    def lhs_of(r, t):
        return jnp.where(t < early(r), 1, 0)

    def remote(src, dst, ss, rs, to):
        return pltpu.make_async_remote_copy(
            src_ref=src, dst_ref=dst, send_sem=ss, recv_sem=rs, device_id=to, device_id_type=MESH
        )

    def forward_hop():
        return remote(out_ref, hb, p_send.at[0], p_recv.at[0], s_to)

    def backward_hop():
        return remote(dh_ref, eb, p_send.at[1], p_recv.at[1], s_to)

    def y_lhs(h):
        return remote(lt.at[2 * other + h], ltr.at[h], y_send.at[tiles + h], y_recv.at[tiles + h], y_to)

    def y_tile(t):
        return remote(ra.at[rhs_of(other, t)], rr.at[t], y_send.at[t], y_recv.at[t], y_to)

    def x_tile(k, t):
        return remote(xs.at[k - 1, t], xr.at[k - 1, t], x_send.at[k - 1, t], x_recv.at[k - 1, t], x_to(k))

    def z_tile(k, t):
        return remote(
            zs.at[t, (hi + k) % n2], zr.at[k - 1, t], z_send.at[k - 1, t], z_recv.at[k - 1, t], z_to(k)
        )

    def g_tile(t):
        return remote(ag.at[rep, t], ag.at[rep, t], g_send.at[t], g_recv.at[t], y_to)

    def small_x(k):
        return remote(sx.at[0], sx.at[k], s_send.at[k - 1], s_recv.at[k - 1], x_to(k))

    def small_z(k):
        n = n1 - 1 + k - 1
        return remote(sz.at[0], sz.at[k], s_send.at[n], s_recv.at[n], z_to(k))

    def small_y():
        n = n1 + n2 - 2
        return remote(sy.at[0], sy.at[1], s_send.at[n], s_recv.at[n], y_to)

    def transpose_into(m, ref):
        for b in range(width // 128):
            block = ref[:, b * 128 : (b + 1) * 128].T
            size = min(shard, 128)
            for q in range(128 // size):
                first = b * 128 + q * size
                j = first // shard
                at = (j // n1) * shard + first % shard
                lt[m, j % n1, at : at + size, :] = block[q * size : (q + 1) * size]

    row_at = lax.broadcasted_iota(jnp.int32, (BLOCK, BLOCK), 0)
    col_at = lax.broadcasted_iota(jnp.int32, (BLOCK, BLOCK), 1)
    base = (row_at // SEG == col_at // SEG) & (col_at <= row_at)
    per = BLOCK // SEG
    for b in range(blocks):
        first = jnp.zeros((BLOCK, BLOCK), jnp.int32)
        for j in range(per):
            first = jnp.where(col_at // SEG == j, SEG - count_ref[b * per + j], first)
        allowed = base & ((col_at % SEG >= first) | (col_at == row_at))
        mask[b] = jnp.where(allowed, 1.0, 0.0)
    acc[...] = jnp.zeros_like(acc)

    LN = 32

    def row_loop(body):
        def run(i, carry):
            body(pl.ds(pl.multiple_of(i * LN, LN), LN))
            return carry

        lax.fori_loop(0, rows // LN, run, 0)

    def tile_loop(count, body):
        def run(t, carry):
            body(t, pl.ds(pl.multiple_of(t * TILE, TILE), TILE))
            return carry

        lax.fori_loop(0, count, run, 0)

    @pl.when(sec == 0)
    def _():
        hb[...] = x_ref[...]

    @pl.when(sec == 1)
    def _():
        eb[...] = ct_ref[...]
        transpose_into(3, eb)

        @pl.when(rep == 0)
        def _():
            y_lhs(1).start()

        forward_hop().wait_recv()

    def first_norm(at):
        normed, inverse = normalize(hb[at].astype(f32))
        norm1[at] = normed
        inv1[at] = inverse
        ab[at] = (normed * gain_ref[0, 0:1] + bias_ref[0, 0:1]).astype(bf16)

    row_loop(first_norm)
    weights[0].wait()

    def project(t, at):
        pb[:, at] = mul(ab[...], wq[:, at]).astype(bf16)

    tile_loop(q_tiles, project)

    def head_loop(body):
        def run(i, carry):
            for b in range(blocks):
                for u in range(2):
                    body(b, 2 * i + u)
            return carry

        lax.fori_loop(0, heads // 2, run, 0)

    def part(b, member, h):
        return pb[b * BLOCK : (b + 1) * BLOCK, pl.ds(pl.multiple_of(member * width + h * HEAD, HEAD), HEAD)]

    def tile_at(first, b, h):
        per_tile = TILE // HEAD
        cols = pl.ds(pl.multiple_of((h % per_tile) * HEAD, HEAD), HEAD)
        return (first + h // per_tile, pl.ds(b * BLOCK, BLOCK), cols)

    def attend(b, h):
        scores = mul(part(b, 0, h), part(b, 1, h), NT) * scale
        scores = jnp.where(mask[b] > 0.5, scores, -1e30)
        raised = jnp.exp(scores - jnp.max(scores, axis=-1, keepdims=True))
        chance = raised * (1.0 / jnp.sum(raised, axis=-1, keepdims=True))
        probs[b, h] = chance
        ra[tile_at(O_AT, b, h)] = mul(chance.astype(bf16), part(b, 2, h)).astype(bf16)

    head_loop(attend)
    weights[1].wait()

    def attention_out(t, at):
        total = hb[:, at].astype(f32)
        for k in range(o_tiles):
            total = total + mul(ra[O_AT + k], wo[k * TILE : (k + 1) * TILE, at])
        mm[:, at] = total

    tile_loop(o_tiles, attention_out)

    def second_norm(at):
        normed, inverse = normalize(mm[at])
        norm2[at] = normed
        inv2[at] = inverse
        cb[at] = (normed * gain_ref[0, 1:2] + bias_ref[0, 1:2]).astype(bf16)

    row_loop(second_norm)
    weights[2].wait()

    def feed_up(t, at):
        upper = mul(cb[...], wu[:, at])
        value, slope = gelu_pair(upper)
        ra[G_AT + t] = value.astype(bf16)
        gp[:, at] = slope

    tile_loop(u_tiles, feed_up)
    weights[3].wait()

    def feed_down(t, at):
        total = mm[:, at]
        for k in range(u_tiles):
            total = total + mul(ra[G_AT + k], wd[k * TILE : (k + 1) * TILE, at])
        out_ref[:, at] = total.astype(bf16)

    tile_loop(o_tiles, feed_down)

    @pl.when(sec == 0)
    def _():
        forward_hop().start()

    transpose_into(2, cb)

    @pl.when(rep == 0)
    def _():
        for t in range(u_tiles):
            y_tile(t).start()
        y_lhs(0).start()

    transpose_into(0, ab)

    @pl.when(rep == 1)
    def _():
        for t in range(o_tiles):
            y_tile(t).start()
        y_lhs(0).start()

    @pl.when(sec == 0)
    def _():
        backward_hop().wait_recv()
        transpose_into(3, eb)

        @pl.when(rep == 0)
        def _():
            y_lhs(1).start()

    def feed_down_back(t, at):
        ra[U_AT + t] = (mul(eb[...], wd[at, :], NT) * gp[:, at]).astype(bf16)

    tile_loop(u_tiles, feed_down_back)

    @pl.when(rep == 0)
    def _():
        for t in range(u_tiles, tiles):
            y_tile(t).start()

    def feed_up_back(t, at):
        total = mul(ra[U_AT], wu[at, 0:TILE], NT)
        for k in range(1, u_tiles):
            total = total + mul(ra[U_AT + k], wu[at, k * TILE : (k + 1) * TILE], NT)
        dcb[:, at] = total

    tile_loop(o_tiles, feed_up_back)

    def add_rows(i, value):
        acc[i] += jnp.sum(value.reshape(LN // 8, 8, width), axis=0)

    def second_back(at):
        d_c, normed = dcb[at], norm2[at]
        add_rows(1, d_c * normed)
        add_rows(3, d_c)
        d_m = eb[at].astype(f32) + normalize_back(d_c * gain_ref[0, 1:2], normed, inv2[at])
        mm[at] = d_m
        dmb[at] = d_m.astype(bf16)

    row_loop(second_back)

    def attention_out_back(t, at):
        dob[:, at] = mul(dmb[...], wo[at, :], NT).astype(bf16)

    tile_loop(o_tiles, attention_out_back)
    transpose_into(1, dmb)

    @pl.when(rep == 1)
    def _():
        y_lhs(1).start()

    def attend_back(b, h):
        d_o = dob[b * BLOCK : (b + 1) * BLOCK, pl.ds(pl.multiple_of(h * HEAD, HEAD), HEAD)]
        q, k, v = part(b, 0, h), part(b, 1, h), part(b, 2, h)
        chance = probs[b, h]
        d_probs = mul(d_o, v, NT)
        d_s = (chance * (d_probs - jnp.sum(chance * d_probs, axis=-1, keepdims=True))).astype(bf16)
        ra[tile_at(0, b, h)] = (mul(d_s, k) * scale).astype(bf16)
        ra[tile_at(o_tiles, b, h)] = (mul(d_s, q, TN) * scale).astype(bf16)
        ra[tile_at(2 * o_tiles, b, h)] = mul(chance.astype(bf16), d_o, TN).astype(bf16)

    head_loop(attend_back)

    @pl.when(rep == 1)
    def _():
        for t in range(o_tiles, tiles):
            y_tile(t).start()

    def project_back(t, at):
        total = mul(ra[0], wq[at, 0:TILE], NT)
        for k in range(1, q_tiles):
            total = total + mul(ra[k], wq[at, k * TILE : (k + 1) * TILE], NT)
        dcb[:, at] = total

    tile_loop(o_tiles, project_back)

    def first_back(at):
        d_a, normed = dcb[at], norm1[at]
        add_rows(0, d_a * normed)
        add_rows(2, d_a)
        d_h = mm[at] + normalize_back(d_a * gain_ref[0, 0:1], normed, inv1[at])
        dh_ref[at] = d_h.astype(bf16)

    row_loop(first_back)

    @pl.when(sec == 1)
    def _():
        backward_hop().start()

    def product(t, which):
        h, r = lhs_of(rep, t), rhs_of(rep, t)
        return mul(lt[2 * rep + h, which], ra[r]) + mul(ltr[h, which], rr[t])

    def stage_a(t):
        for h in range(2):

            @pl.when(t == (0 if h == 1 else early(rep)))
            def _():
                y_lhs(h).wait_recv()

        y_tile(t).wait_recv()
        for k in range(1, n1):
            part_sum = product(t, (lo + k) % n1).astype(bf16)
            for q in range(n2):
                xs[k - 1, t, q] = part_sum[q * shard : (q + 1) * shard]
            x_tile(k, t).start()

    def stage_b(t):
        part_sum = product(t, lo)
        for k in range(1, n1):
            x_tile(k, t).wait_recv()
        for q in range(n2):
            total = part_sum[q * shard : (q + 1) * shard]
            for k in range(1, n1):
                total = total + xr[k - 1, t, q].astype(f32)
            zs[t, q] = total.astype(bf16)

            @pl.when(hi == q)
            def _():
                own[t] = total

        for k in range(1, n2):
            z_tile(k, t).start()

    def stage_c(t):
        total = own[t]
        for k in range(1, n2):
            z_tile(k, t).wait_recv()
            total = total + zr[k - 1, t].astype(f32)
        ag[rep, t] = total.astype(bf16)
        g_tile(t).start()

    def reduce_step(s, carry):
        for lag, stage in ((0, stage_a), (2, stage_b), (4, stage_c)):

            @pl.when((s >= lag) & (s < tiles + lag))
            def _():
                stage(s - lag)

        return carry

    lax.fori_loop(0, tiles + 4, reduce_step, 0)

    for i in range(4):
        sx[0, i : i + 1] = jnp.sum(acc[i], axis=0, keepdims=True)
        sx[0, 4 + i : 5 + i] = jnp.zeros((1, width), f32)
    for k in range(1, n1):
        small_x(k).start()
    total = sx[0]
    for k in range(1, n1):
        small_x(k).wait_recv()
        total = total + sx[k]
    sz[0] = total
    for k in range(1, n2):
        small_z(k).start()
    for k in range(1, n2):
        small_z(k).wait_recv()
        total = total + sz[k]
    sy[0] = total
    small_y().start()
    small_y().wait_recv()
    sy[2] = sy[0] + sy[1]
    if shard % 128 == 0:
        small_ref[...] = sy[2, :, pl.ds(pl.multiple_of(me * shard, shard), shard)]
    else:
        small_ref[...] = sy[2]

    for t in range(tiles):
        g_tile(t).wait_recv()
        c = (t + tiles - o_tiles) % tiles
        if c < q_tiles:
            gq_ref[:, c * TILE : (c + 1) * TILE] = ag[0, t]
        elif shard % 128 == 0:
            go_ref[(c - q_tiles) * TILE : (c - q_tiles + 1) * TILE, :] = ag[0, t].T
        else:
            go_ref[:, (c - q_tiles) * TILE : (c - q_tiles + 1) * TILE] = ag[0, t]
        c = (t + tiles - u_tiles) % tiles
        if c < u_tiles:
            gu_ref[:, c * TILE : (c + 1) * TILE] = ag[1, t]
        elif shard % 128 == 0:
            gd_ref[(c - u_tiles) * TILE : (c - u_tiles + 1) * TILE, :] = ag[1, t].T
        else:
            gd_ref[:, (c - u_tiles) * TILE : (c - u_tiles + 1) * TILE] = ag[1, t]

    def drain(t, carry):
        y_tile(t).wait_send()
        for k in range(1, n1):
            x_tile(k, t).wait_send()
        for k in range(1, n2):
            z_tile(k, t).wait_send()
        g_tile(t).wait_send()
        return carry

    lax.fori_loop(0, tiles, drain, 0)
    for h in range(2):
        y_lhs(h).wait_send()
    for k in range(1, n1):
        small_x(k).wait_send()
    for k in range(1, n2):
        small_z(k).wait_send()
    small_y().wait_send()

    @pl.when(sec == 0)
    def _():
        forward_hop().wait_send()

    @pl.when(sec == 1)
    def _():
        backward_hop().wait_send()


def per_device(inputs, cotangent, seg_counts, w_qkv, w_out, w_up, w_down, gains, biases):
    dp = lax.axis_size("dp")
    n1 = 2 if dp < 16 else 4
    n2 = dp // n1
    rows, width = inputs.shape
    ff = w_up.shape[2]
    shard = width // dp
    direct = shard % 128 == 0
    tiles = 2 * ff // TILE
    blocks, heads = rows // BLOCK, width // HEAD
    o_tiles = width // TILE
    dma = pltpu.SemaphoreType.DMA
    vm = pltpu.VMEM
    act = vm((rows, width), bf16)
    wide = vm((rows, width), f32)
    scratch = [
        vm((width, 3 * width), bf16), vm((width, width), bf16), vm((width, ff), bf16), vm((ff, width), bf16),
        act, act, wide, wide, vm((rows, 1), f32), vm((rows, 1), f32),
        act, vm((rows, 3 * width), bf16), act, act, act,
        vm((blocks, heads, BLOCK, BLOCK), f32), wide, vm((rows, ff), f32), wide,
        vm((4, 8, width), f32), vm((blocks, BLOCK, BLOCK), f32),
        vm((4, n1, n2 * shard, rows), bf16),
        vm((2, n1, n2 * shard, rows), bf16),
        vm((2 * tiles, rows, TILE), bf16),
        vm((tiles, rows, TILE), bf16),
        vm((n1 - 1, tiles, n2, shard, TILE), bf16),
        vm((n1 - 1, tiles, n2, shard, TILE), bf16),
        vm((tiles, n2, shard, TILE), bf16),
        vm((n2 - 1, tiles, shard, TILE), bf16),
        vm((tiles, shard, TILE), f32),
        vm((2, tiles, shard, TILE), bf16),
        vm((n1, 8, width), f32), vm((n2, 8, width), f32), vm((3, 8, width), f32),
        dma((4,)),
        dma((tiles + 2,)), dma((tiles + 2,)),
        dma((n1 - 1, tiles)), dma((n1 - 1, tiles)),
        dma((n2 - 1, tiles)), dma((n2 - 1, tiles)),
        dma((tiles,)), dma((tiles,)),
        dma((n1 + n2 - 1,)), dma((n1 + n2 - 1,)),
        dma((2,)), dma((2,)),
    ]
    vspec = pl.BlockSpec(memory_space=pltpu.VMEM)
    hbm = pl.BlockSpec(memory_space=pl.ANY)
    sds = jax.ShapeDtypeStruct
    turned = (lambda n: (n, shard)) if direct else (lambda n: (shard, n))
    out, d_h, g_q, g_o, g_u, g_d, small = pl.pallas_call(
        partial(step_kernel, n1, n2),
        out_shape=(
            sds((rows, width), bf16), sds((rows, width), bf16),
            sds((shard, 3 * width), bf16), sds(turned(width), bf16),
            sds((shard, ff), bf16), sds(turned(ff), bf16),
            sds((8, shard if direct else width), f32),
        ),
        in_specs=[vspec, vspec, pl.BlockSpec(memory_space=pltpu.SMEM)] + [hbm] * 4 + [vspec] * 2,
        out_specs=(vspec,) * 7,
        scratch_shapes=scratch,
        name="layers_step",
        compiler_params=pltpu.CompilerParams(
            collective_id=0, has_side_effects=True, vmem_limit_bytes=67043328
        ),
    )(inputs, cotangent, seg_counts, w_qkv, w_out, w_up, w_down, gains, biases)
    if not direct:
        g_o, g_d = g_o.T, g_d.T
        small = lax.dynamic_slice_in_dim(small, lax.axis_index("dp") * shard, shard, 1)
    grads = [g.astype(f32)[None] for g in (g_q, g_o, g_u, g_d)]
    return (out[None], d_h[None], *grads, small[None, 0:2], small[None, 2:4])


def solution(mesh):
    rows = P(("dp", "rep"), None)
    layer = P("section", None, None)
    return jax.shard_map(
        per_device,
        mesh=mesh,
        in_specs=(rows, rows, P(("dp", "rep"))) + (layer,) * 6,
        out_specs=(
            P("section", ("dp", "rep"), None),
            P("section", ("dp", "rep"), None),
            P("section", "dp", None),
            P("section", None, "dp"),
            P("section", "dp", None),
            P("section", None, "dp"),
            P("section", None, "dp"),
            P("section", None, "dp"),
        ),
        check_vma=False,
    )
```

```python
from functools import partial

import jax
import jax.numpy as jnp
from jax import lax
from jax.experimental import pallas as pl
from jax.experimental.pallas import tpu as pltpu
from jax.sharding import PartitionSpec as P

SEG = 16
HEAD = 128
BLOCK = 128
TILE = 512
CUT = 256
MESH = pl.DeviceIdType.MESH
epsilon = 1e-05
f32 = jnp.float32
bf16 = jnp.bfloat16
NN = (((1,), (0,)), ((), ()))
NT = (((1,), (1,)), ((), ()))
TN = (((0,), (0,)), ((), ()))


def mul(left, right, dims=NN):
    return lax.dot_general(left, right, dims, preferred_element_type=f32)


def normalize(hidden):
    average = jnp.mean(hidden, axis=-1, keepdims=True)
    centred = hidden - average
    inverse = lax.rsqrt(jnp.mean(centred * centred, axis=-1, keepdims=True) + epsilon)
    return (centred * inverse, inverse)


def normalize_back(grad_normed, normed, inverse):
    centre_term = jnp.mean(grad_normed, axis=-1, keepdims=True)
    slope_term = normed * jnp.mean(grad_normed * normed, axis=-1, keepdims=True)
    return inverse * (grad_normed - centre_term - slope_term)


def gelu_pair(u):
    k = 0.7978845608
    square = u * u
    t = jnp.tanh(k * (u + 0.044715 * u * square))
    half = 0.5 * (1.0 + t)
    slope = half + 0.5 * u * (1.0 - t * t) * (k * (1.0 + 3 * 0.044715 * square))
    return u * half, slope


def step_kernel(
    x_hbm, ct_hbm, count_ref, wq_hbm, wo_hbm, wu_hbm, wd_hbm, gain_ref, bias_ref,
    out_hbm, dh_hbm, grad_hbm, small_ref,
    wq, wo, wu, wd, hb, eb, norm1, norm2, inv1, inv2, ab, pb, cb, dmb, dob, probs, mm, gp, dcb, acc, mask,
    mask2, pin, out_ref, dh_ref, lt, ltr, ra, rr, ag, small, *rest,
):
    dp = lt.shape[1] * lt.shape[2]
    levels = dp.bit_length() - 1
    sends, arrivals = rest[:levels], rest[levels : 2 * levels]
    w_sem, o_sem, y_send, y_recv, x_send, x_recv, g_send, g_recv, s_send, s_recv, p_send, p_recv = rest[2 * levels :]
    rows, width = hb.shape
    blocks = rows // BLOCK
    heads = width // HEAD
    ff = wu.shape[1]
    shard = width // dp
    tiles = ra.shape[0] // 2
    cuts = ag.shape[1]
    per_tile = cuts // tiles
    scale = HEAD**-0.5
    sec = lax.axis_index("section")
    me = lax.axis_index("dp")
    rep = lax.axis_index("rep")
    other = 1 - rep
    y_to = (sec, me, other)
    s_to = (1 - sec, me, rep)

    def x_to(bit):
        stride = 1 << bit
        return (sec, me + stride - 2 * stride * (me // stride % 2), rep)

    weights = [
        pltpu.make_async_copy(src.at[0], dst, w_sem.at[i])
        for i, (src, dst) in enumerate(((wq_hbm, wq), (wo_hbm, wo), (wu_hbm, wu), (wd_hbm, wd)))
    ]
    take_x = pltpu.make_async_copy(x_hbm, hb, o_sem.at[3])
    take_ct = pltpu.make_async_copy(ct_hbm, eb, o_sem.at[3])

    @pl.when(sec == 0)
    def _():
        take_x.start()

    @pl.when(sec == 1)
    def _():
        take_ct.start()

    for copy in weights:
        copy.start()

    barrier = pltpu.get_barrier_semaphore()
    peers = [s_to, y_to] + [x_to(bit) for bit in range(levels)]
    for peer in peers:
        pl.semaphore_signal(barrier, inc=1, device_id=peer, device_id_type=MESH)
    pl.semaphore_wait(barrier, len(peers))

    q_tiles, o_tiles, u_tiles = 3 * width // TILE, width // TILE, ff // TILE
    O_AT, U_AT, G_AT = q_tiles, tiles, tiles + u_tiles

    def early(r):
        return jnp.where(r == 0, o_tiles, u_tiles)

    def rhs_of(r, t):
        return r * tiles + (t + tiles - early(r)) % tiles

    def lhs_of(r, t):
        return jnp.where(t < early(r), 1, 0)

    def remote(src, dst, ss, rs, to):
        return pltpu.make_async_remote_copy(
            src_ref=src, dst_ref=dst, send_sem=ss, recv_sem=rs, device_id=to, device_id_type=MESH
        )

    def forward_hop():
        return remote(out_ref, hb, p_send.at[0], p_recv.at[0], s_to)

    def backward_hop():
        return remote(dh_ref, eb, p_send.at[1], p_recv.at[1], s_to)

    def y_hop(n, src, dst):
        return remote(src, dst, y_send.at[n], y_recv.at[n], y_to)

    def y_act(h, src):
        return y_hop(h, src, pin.at[h])

    def y_mask():
        return y_hop(2, mask, mask2)

    def y_mixed(t):
        return y_hop(3 + t, ra.at[O_AT + t], rr.at[t])

    def bit_of(level, t):
        return jnp.where(t % 3 == 2, 1 - level, level) if level < 2 else level

    def half_of(level, t):
        return me // (1 << bit_of(level, t)) % 2 if level >= 2 else jnp.where(bit_of(level, t) == 0, me % 2, me // 2 % 2)

    def peer_of(level, t):
        stride = jnp.where(bit_of(level, t) == 0, 1, 2) if level < 2 else 1 << level
        return (sec, me + stride - 2 * stride * half_of(level, t), rep)

    def x_tile(level, t):
        return remote(
            sends[level].at[t, 1 - half_of(level, t)] if level else sends[0].at[t],
            arrivals[level].at[t], x_send.at[level, t], x_recv.at[level, t], peer_of(level, t),
        )

    def g_tile(t):
        return remote(ag.at[rep, t], ag.at[rep, t], g_send.at[t], g_recv.at[t], y_to)

    def small_hop(n):
        to = x_to(n) if n < levels else y_to
        return remote(small.at[2 * n], small.at[2 * n + 1], s_send.at[n], s_recv.at[n], to)

    def transpose_into(lt, m, ref):
        for b in range(width // 128):
            block = ref[:, b * 128 : (b + 1) * 128].T
            size = min(shard, 128)
            for q in range(128 // size):
                first = b * 128 + q * size
                j = first // shard
                lt[m, j % 2, j // 2, first % shard : first % shard + size, :] = block[q * size : (q + 1) * size]

    row_at = lax.broadcasted_iota(jnp.int32, (BLOCK, BLOCK), 0)
    col_at = lax.broadcasted_iota(jnp.int32, (BLOCK, BLOCK), 1)
    base = (row_at // SEG == col_at // SEG) & (col_at <= row_at)
    per = BLOCK // SEG
    for b in range(blocks):
        first = jnp.zeros((BLOCK, BLOCK), jnp.int32)
        for j in range(per):
            first = jnp.where(col_at // SEG == j, SEG - count_ref[b * per + j], first)
        allowed = base & ((col_at % SEG >= first) | (col_at == row_at))
        mask[b] = jnp.where(allowed, 1.0, 0.0)
    acc[...] = jnp.zeros_like(acc)

    LN = 128

    def row_loop(body):
        def run(i, carry):
            body(pl.ds(pl.multiple_of(i * LN, LN), LN))
            return carry

        lax.fori_loop(0, rows // LN, run, 0)

    def tile_loop(count, body):
        def run(t, carry):
            body(t, pl.ds(pl.multiple_of(t * TILE, TILE), TILE))
            return carry

        lax.fori_loop(0, count, run, 0)

    y_mask().start()

    def share_grad():
        @pl.when(rep == 0)
        def _():
            y_act(1, eb).start()

        @pl.when(rep == 1)
        def _():
            transpose_into(lt, 1, eb)

    @pl.when(sec == 0)
    def _():
        take_x.wait()

    @pl.when(sec == 1)
    def _():
        take_ct.wait()
        share_grad()
        forward_hop().wait_recv()

    def first_norm(at):
        normed, inverse = normalize(hb[at].astype(f32))
        norm1[at] = normed
        inv1[at] = inverse
        ab[at] = (normed * gain_ref[0, 0:1] + bias_ref[0, 0:1]).astype(bf16)

    row_loop(first_norm)

    @pl.when(rep == 1)
    def _():
        y_act(0, ab).start()

    weights[0].wait()

    def project(source):
        def run(t, at):
            pb[:, at] = mul(source(), wq[:, at]).astype(bf16)

        tile_loop(q_tiles, run)

    project(lambda: ab[...])

    def head_loop(body):
        def run(i, carry):
            body([(b, i * 8 + u) for u in range(8) for b in range(blocks)])
            return carry

        lax.fori_loop(0, heads // 8, run, 0)

    def part(b, member, h):
        return pb[b * BLOCK : (b + 1) * BLOCK, pl.ds(pl.multiple_of(member * width + h * HEAD, HEAD), HEAD)]

    def tile_at(first, b, h):
        group = TILE // HEAD
        cols = pl.ds(pl.multiple_of((h % group) * HEAD, HEAD), HEAD)
        return (first + h // group, pl.ds(b * BLOCK, BLOCK), cols)

    def chances_of(pairs, mask):
        scores = [mul(part(b, 0, h), part(b, 1, h), NT) for b, h in pairs]
        chances = []
        for (b, h), score in zip(pairs, scores):
            score = jnp.where(mask[b] > 0.5, score * scale, -1e30)
            raised = jnp.exp(score - jnp.max(score, axis=-1, keepdims=True))
            chance = raised * (1.0 / jnp.sum(raised, axis=-1, keepdims=True))
            probs[b, h] = chance
            chances.append(chance.astype(bf16))
        return chances

    def attend(pairs):
        for (b, h), chance in zip(pairs, chances_of(pairs, mask)):
            ra[tile_at(O_AT, b, h)] = mul(chance, part(b, 2, h)).astype(bf16)

    head_loop(attend)

    @pl.when(rep == 1)
    def _():
        for t in range(o_tiles):
            y_mixed(t).start()

    weights[1].wait()

    def attention_out(t, at):
        total = hb[:, at].astype(f32)
        for k in range(o_tiles):
            total = total + mul(ra[O_AT + k], wo[k * TILE : (k + 1) * TILE, at])
        mm[:, at] = total

    tile_loop(o_tiles, attention_out)

    def second_norm(at):
        normed, inverse = normalize(mm[at])
        norm2[at] = normed
        inv2[at] = inverse
        cb[at] = (normed * gain_ref[0, 1:2] + bias_ref[0, 1:2]).astype(bf16)

    row_loop(second_norm)

    @pl.when(rep == 0)
    def _():
        y_act(0, cb).start()

    weights[2].wait()

    def feed_up(t, at, source, store, first):
        value, slope = gelu_pair(mul(source[...], wu[:, at]))
        store[first + t] = value.astype(bf16)
        gp[:, at] = slope

    tile_loop(u_tiles, partial(feed_up, source=cb, store=ra, first=G_AT))
    weights[3].wait()

    def feed_down(t, at):
        total = mm[:, at]
        for k in range(u_tiles):
            total = total + mul(ra[G_AT + k], wd[k * TILE : (k + 1) * TILE, at])
        out_ref[:, at] = total.astype(bf16)

    tile_loop(o_tiles, feed_down)

    @pl.when(sec == 0)
    def _():
        forward_hop().start()

    out_copy = pltpu.make_async_copy(out_ref, out_hbm, o_sem.at[0])
    out_copy.start()

    @pl.when(rep == 0)
    def _():
        transpose_into(lt, 0, ab)

    @pl.when(rep == 1)
    def _():
        transpose_into(lt, 0, cb)

    @pl.when(sec == 0)
    def _():
        backward_hop().wait_recv()
        share_grad()

    def piece(v, j, t):
        alt = t % 3 == 2
        return jnp.where(alt, j % 2, v), jnp.where(alt, j // 2 * 2 + v, j)

    def product(t, v):
        tile = t // per_tile
        cols = pl.ds(pl.multiple_of(t % per_tile * CUT, CUT), CUT)
        h, r = lhs_of(rep, tile), rhs_of(rep, tile)
        places = [piece(v, j, t) for j in range(dp // 2)]
        mine = jnp.concatenate([lt[h, a, b] for a, b in places], axis=0)
        theirs = jnp.concatenate([ltr[h, a, b] for a, b in places], axis=0)
        return mul(mine, ra[r, :, cols]) + mul(theirs, rr[tile, :, cols])

    def open_tile(t):
        part_sum = product(t, 1 - half_of(0, t)).astype(bf16)
        for j in range(dp // 2):
            sends[0][t, j] = part_sum[j * shard : (j + 1) * shard]
        x_tile(0, t).start()

    def open_range(first, last):
        def run(t, carry):
            open_tile(t)
            return carry

        lax.fori_loop(first, last, run, 0)

    def merge(level, t):
        count = dp >> (level + 1)
        if level == 0:
            part_sum = product(t, half_of(0, t))
            x_tile(0, t).wait_recv()
            kept = [part_sum[j * shard : (j + 1) * shard] for j in range(count)]
        else:
            x_tile(level, t).wait_recv()
            kept = [sends[level][t, half_of(level, t), j].astype(f32) for j in range(count)]
        for j in range(count):
            total = (kept[j] + arrivals[level][t, j].astype(f32)).astype(bf16)
            if level + 1 < levels:
                sends[level + 1][t, j % 2, j // 2] = total
            else:
                ag[rep, t] = total
        if level + 1 < levels:
            x_tile(level + 1, t).start()
        else:
            g_tile(t).start()

    def feed_down_back(t, at, source, store, first):
        store[first + t] = (mul(source[...], wd[at, :], NT) * gp[:, at]).astype(bf16)

    tile_loop(u_tiles, partial(feed_down_back, source=eb, store=ra, first=U_AT))

    @pl.when(rep == 1)
    def _():
        y_act(0, cb).wait_recv()
        transpose_into(ltr, 0, pin.at[0])
        y_act(1, eb).wait_recv()
        transpose_into(ltr, 1, pin.at[1])

        def run(t, at):
            feed_up(t, at, pin.at[0], rr, 0)
            open_range(t * per_tile, (t + 1) * per_tile)

        tile_loop(u_tiles, run)

    def feed_up_back(t, at):
        total = mul(ra[U_AT], wu[at, 0:TILE], NT)
        for k in range(1, u_tiles):
            total = total + mul(ra[U_AT + k], wu[at, k * TILE : (k + 1) * TILE], NT)
        dcb[:, at] = total

    tile_loop(o_tiles, feed_up_back)

    def add_rows(i, value):
        acc[i] += jnp.sum(value.reshape(LN // 8, 8, width), axis=0)

    def second_back(at):
        d_c, normed = dcb[at], norm2[at]
        add_rows(1, d_c * normed)
        add_rows(3, d_c)
        d_m = eb[at].astype(f32) + normalize_back(d_c * gain_ref[0, 1:2], normed, inv2[at])
        mm[at] = d_m
        dmb[at] = d_m.astype(bf16)

    row_loop(second_back)

    @pl.when(rep == 1)
    def _():
        y_act(1, dmb).start()

    def attention_out_back(t, at, source):
        dob[:, at] = mul(source[...], wo[at, :], NT).astype(bf16)

    tile_loop(o_tiles, partial(attention_out_back, source=dmb))

    @pl.when(rep == 0)
    def _():
        transpose_into(lt, 1, dmb)

    def attend_back(pairs, store, first):
        def d_out(b, h):
            return dob[b * BLOCK : (b + 1) * BLOCK, pl.ds(pl.multiple_of(h * HEAD, HEAD), HEAD)]

        d_chances = [mul(d_out(b, h), part(b, 2, h), NT) for b, h in pairs]
        for b, h in pairs:
            store[tile_at(first + 2 * o_tiles, b, h)] = mul(probs[b, h].astype(bf16), d_out(b, h), TN).astype(bf16)
        d_scores = []
        for (b, h), d_probs in zip(pairs, d_chances):
            chance = probs[b, h]
            inner = jnp.sum(chance * d_probs, axis=-1, keepdims=True)
            d_scores.append((chance * (d_probs - inner)).astype(bf16))
        for (b, h), d_s in zip(pairs, d_scores):
            store[tile_at(first, b, h)] = (mul(d_s, part(b, 1, h)) * scale).astype(bf16)
        for (b, h), d_s in zip(pairs, d_scores):
            store[tile_at(first + o_tiles, b, h)] = (mul(d_s, part(b, 0, h), TN) * scale).astype(bf16)

    head_loop(partial(attend_back, store=ra, first=0))

    def project_back(t, at):
        total = mul(ra[0], wq[at, 0:TILE], NT)
        for k in range(1, q_tiles):
            total = total + mul(ra[k], wq[at, k * TILE : (k + 1) * TILE], NT)
        dcb[:, at] = total

    tile_loop(o_tiles, project_back)

    def first_back(at):
        d_a, normed = dcb[at], norm1[at]
        add_rows(0, d_a * normed)
        add_rows(2, d_a)
        d_h = mm[at] + normalize_back(d_a * gain_ref[0, 0:1], normed, inv1[at])
        dh_ref[at] = d_h.astype(bf16)

    row_loop(first_back)

    @pl.when(sec == 1)
    def _():
        backward_hop().start()

    dh_copy = pltpu.make_async_copy(dh_ref, dh_hbm, o_sem.at[1])
    dh_copy.start()

    @pl.when(rep == 0)
    def _():
        y_act(0, ab).wait_recv()
        transpose_into(ltr, 0, pin.at[0])
        y_act(1, dmb).wait_recv()
        transpose_into(ltr, 1, pin.at[1])
        for t in range(o_tiles):
            y_mixed(t).wait_recv()
        open_range(0, o_tiles * per_tile)
        project(lambda: pin[0])
        y_mask().wait_recv()
        head_loop(partial(chances_of, mask=mask2))
        tile_loop(o_tiles, partial(attention_out_back, source=pin.at[1]))
        head_loop(partial(attend_back, store=rr, first=o_tiles))

    @pl.when(rep == 1)
    def _():
        y_mask().wait_recv()
        tile_loop(u_tiles, partial(feed_down_back, source=pin.at[1], store=rr, first=u_tiles))


    for i in range(4):
        small[0, i : i + 1] = jnp.sum(acc[i], axis=0, keepdims=True)
        small[0, 4 + i : 5 + i] = jnp.zeros((1, width), f32)
    small_hop(0).start()

    def small_merge(n):
        small_hop(n).wait_recv()
        small[2 * n + 2] = small[2 * n] + small[2 * n + 1]
        if n < levels:
            small_hop(n + 1).start()

    lags = [2 + 3 * level for level in range(levels)]
    opened = jnp.where(rep == 0, o_tiles * per_tile, (u_tiles * per_tile))

    def reduce_step(s, carry):
        @pl.when(s + opened < cuts)
        def _():
            open_tile(s + opened)

        for level, lag in enumerate(lags):

            @pl.when((s >= lag) & (s < cuts + lag))
            def _():
                merge(level, s - lag)

        for n in range(levels + 1):

            @pl.when(s == 2 * n + 2)
            def _():
                small_merge(n)

        return carry

    lax.fori_loop(0, cuts + lags[-1], reduce_step, 0)

    if shard % 128 == 0:
        small_ref[...] = small[2 * levels + 2, :, pl.ds(pl.multiple_of(me * shard, shard), shard)]
    else:
        small_ref[...] = small[2 * levels + 2]

    def drain(t, carry):
        g_tile(t).wait_recv()
        for level in range(levels):
            x_tile(level, t).wait_send()
        g_tile(t).wait_send()
        return carry

    lax.fori_loop(0, cuts, drain, 0)
    grads_copy = pltpu.make_async_copy(ag, grad_hbm, o_sem.at[2])
    grads_copy.start()
    y_mask().wait_send()
    for h in range(2):
        y_act(h, eb).wait_send()

    @pl.when(rep == 1)
    def _():
        for t in range(o_tiles):
            y_mixed(t).wait_send()

    for n in range(levels + 1):
        small_hop(n).wait_send()

    @pl.when(sec == 0)
    def _():
        forward_hop().wait_send()

    @pl.when(sec == 1)
    def _():
        backward_hop().wait_send()

    out_copy.wait()
    dh_copy.wait()
    grads_copy.wait()


def finish_kernel(near, turn, grad_ref, out_ref, dh_ref, gq, go, gu, gd, out, dh):
    t = pl.program_id(0)

    for r, first, second in ((0, go, gq), (1, gd, gu)):
        for c in range(grad_ref.shape[1]):
            at = slice(c * CUT, (c + 1) * CUT)

            @pl.when(t < near[r])
            def _():
                if turn:
                    first[0, at, :] = grad_ref[r, c].T.astype(f32)
                else:
                    first[0, :, at] = grad_ref[r, c].astype(f32)

            @pl.when(t >= near[r])
            def _():
                second[0, :, at] = grad_ref[r, c].astype(f32)

    out[0] = out_ref[...]
    dh[0] = dh_ref[...]


def per_device(inputs, cotangent, seg_counts, w_qkv, w_out, w_up, w_down, gains, biases):
    dp = lax.axis_size("dp")
    levels = dp.bit_length() - 1
    rows, width = inputs.shape
    ff = w_up.shape[2]
    shard = width // dp
    whole_lanes = shard % 128 == 0
    tiles = 2 * ff // TILE
    cuts = tiles * TILE // CUT
    q_tiles, o_tiles, u_tiles = 3 * width // TILE, width // TILE, ff // TILE
    blocks, heads = rows // BLOCK, width // HEAD
    dma = pltpu.SemaphoreType.DMA
    vm = pltpu.VMEM
    act = vm((rows, width), bf16)
    wide = vm((rows, width), f32)
    scratch = [
        vm((width, 3 * width), bf16), vm((width, width), bf16), vm((width, ff), bf16), vm((ff, width), bf16),
        act, act, wide, wide, vm((rows, 1), f32), vm((rows, 1), f32),
        act, vm((rows, 3 * width), bf16), act, act, act,
        vm((blocks, heads, BLOCK, BLOCK), f32), wide, vm((rows, ff), f32), wide,
        vm((4, 8, width), f32), vm((blocks, BLOCK, BLOCK), f32),
        vm((blocks, BLOCK, BLOCK), f32), vm((2, rows, width), bf16),
        act, act,
        vm((2, 2, dp // 2, shard, rows), bf16),
        vm((2, 2, dp // 2, shard, rows), bf16),
        vm((2 * tiles, rows, TILE), bf16),
        vm((tiles, rows, TILE), bf16),
        vm((2, cuts, shard, CUT), bf16),
        vm((2 * levels + 3, 8, width), f32),
        vm((cuts, dp // 2, shard, CUT), bf16),
        *[vm((cuts, 2, dp >> (level + 1), shard, CUT), bf16) for level in range(1, levels)],
        *[vm((cuts, dp >> (level + 1), shard, CUT), bf16) for level in range(levels)],
        dma((4,)), dma((4,)),
        dma((3 + o_tiles,)), dma((3 + o_tiles,)),
        dma((levels, cuts)), dma((levels, cuts)),
        dma((cuts,)), dma((cuts,)),
        dma((levels + 1,)), dma((levels + 1,)),
        dma((2,)), dma((2,)),
    ]
    vspec = pl.BlockSpec(memory_space=pltpu.VMEM)
    hbm = pl.BlockSpec(memory_space=pl.ANY)
    sds = jax.ShapeDtypeStruct
    out, d_h, grads, small = pl.pallas_call(
        step_kernel,
        out_shape=(
            sds((rows, width), bf16), sds((rows, width), bf16),
            sds((2, cuts, shard, CUT), bf16),
            sds((8, shard if whole_lanes else width), f32),
        ),
        in_specs=[hbm, hbm, pl.BlockSpec(memory_space=pltpu.SMEM)] + [hbm] * 4 + [vspec] * 2,
        out_specs=(hbm, hbm, hbm, vspec),
        scratch_shapes=scratch,
        name="layers_step",
        compiler_params=pltpu.CompilerParams(
            collective_id=0, has_side_effects=True, vmem_limit_bytes=67043328
        ),
    )(inputs, cotangent, seg_counts, w_qkv, w_out, w_up, w_down, gains, biases)

    def turned(n, near):
        if whole_lanes:
            return sds((1, n, shard), f32), pl.BlockSpec((1, width, shard), lambda t: (0, jnp.minimum(t, near - 1), 0))
        return sds((1, shard, n), f32), pl.BlockSpec((1, shard, width), lambda t: (0, 0, jnp.minimum(t, near - 1)))

    def flat(n, near):
        return sds((1, shard, n), f32), pl.BlockSpec((1, shard, width), lambda t: (0, 0, jnp.maximum(t - near, 0)))

    steps = 2 * ff // width
    near = (1, ff // width)
    step = rows // steps
    copied = sds((1, rows, width), bf16), pl.BlockSpec((1, step, width), lambda t: (0, t, 0))
    shapes = (flat(3 * width, near[0]), turned(width, near[0]), flat(ff, near[1]), turned(ff, near[1]), copied, copied)
    by_rows = pl.BlockSpec((step, width), lambda t: (t, 0))
    g_q, g_o, g_u, g_d, out, d_h = pl.pallas_call(
        partial(finish_kernel, near, whole_lanes),
        grid=(steps,),
        out_shape=[shape for shape, _ in shapes],
        in_specs=[pl.BlockSpec((2, cuts // steps, shard, CUT), lambda t: (0, t, 0, 0)), by_rows, by_rows],
        out_specs=[spec for _, spec in shapes],
        name="finish",
    )(grads, out, d_h)
    if not whole_lanes:
        g_o, g_d = jnp.swapaxes(g_o, 1, 2), jnp.swapaxes(g_d, 1, 2)
        small = lax.dynamic_slice_in_dim(small, lax.axis_index("dp") * shard, shard, 1)
    return (out, d_h, g_q, g_o, g_u, g_d, small[None, 0:2], small[None, 2:4])


def solution(mesh):
    rows = P(("dp", "rep"), None)
    layer = P("section", None, None)
    return jax.shard_map(
        per_device,
        mesh=mesh,
        in_specs=(rows, rows, P(("dp", "rep"))) + (layer,) * 6,
        out_specs=(
            P("section", ("dp", "rep"), None),
            P("section", ("dp", "rep"), None),
            P("section", "dp", None),
            P("section", None, "dp"),
            P("section", "dp", None),
            P("section", None, "dp"),
            P("section", None, "dp"),
            P("section", None, "dp"),
        ),
        check_vma=False,
    )
```

```python
from functools import partial

import jax
import jax.numpy as jnp
from jax import lax
from jax.experimental import pallas as pl
from jax.experimental.pallas import tpu as pltpu
from jax.sharding import PartitionSpec as P

SEG = 16
HEAD = 128
BLOCK = 128
TILE = 512
CUT = 256
MESH = pl.DeviceIdType.MESH
epsilon = 1e-05
f32 = jnp.float32
bf16 = jnp.bfloat16
NN = (((1,), (0,)), ((), ()))
NT = (((1,), (1,)), ((), ()))
TN = (((0,), (0,)), ((), ()))


def mul(left, right, dims=NN):
    return lax.dot_general(left, right, dims, preferred_element_type=f32)


def normalize(hidden):
    average = jnp.mean(hidden, axis=-1, keepdims=True)
    centred = hidden - average
    inverse = lax.rsqrt(jnp.mean(centred * centred, axis=-1, keepdims=True) + epsilon)
    return (centred * inverse, inverse)


def normalize_back(grad_normed, normed, inverse):
    centre_term = jnp.mean(grad_normed, axis=-1, keepdims=True)
    slope_term = normed * jnp.mean(grad_normed * normed, axis=-1, keepdims=True)
    return inverse * (grad_normed - centre_term - slope_term)


def gelu_pair(u):
    k = 0.7978845608
    square = u * u
    t = jnp.tanh(k * (u + 0.044715 * u * square))
    half = 0.5 * (1.0 + t)
    slope = half + 0.5 * u * (1.0 - t * t) * (k * (1.0 + 3 * 0.044715 * square))
    return u * half, slope


def step_kernel(
    x_hbm, ct_hbm, count_ref, wq_hbm, wo_hbm, wu_hbm, wd_hbm, gain_ref, bias_ref,
    out_hbm, dh_hbm, grad_hbm, small_ref,
    wq, wo, wu, wd, hb, eb, norm1, norm2, inv1, inv2, ab, pb, cb, dmb, dob, probs, mm, gp, dcb, acc, mask,
    mask2, pin, out_ref, dh_ref, lt, ltr, ra, rr, ag, small, *rest,
):
    dp = lt.shape[1] * lt.shape[2]
    levels = dp.bit_length() - 1
    sends, arrivals = rest[:levels], rest[levels : 2 * levels]
    w_sem, o_sem, y_send, y_recv, x_send, x_recv, g_send, g_recv, s_send, s_recv, p_send, p_recv = rest[2 * levels :]
    rows, width = hb.shape
    blocks = rows // BLOCK
    heads = width // HEAD
    ff = wu.shape[1]
    shard = width // dp
    tiles = ra.shape[0] // 2
    cuts = ag.shape[1]
    per_tile = cuts // tiles
    scale = HEAD**-0.5
    sec = lax.axis_index("section")
    me = lax.axis_index("dp")
    rep = lax.axis_index("rep")
    other = 1 - rep
    y_to = (sec, me, other)
    s_to = (1 - sec, me, rep)

    def x_to(bit):
        stride = 1 << bit
        return (sec, me + stride - 2 * stride * (me // stride % 2), rep)

    weights = [
        pltpu.make_async_copy(src.at[0], dst, w_sem.at[i])
        for i, (src, dst) in enumerate(((wq_hbm, wq), (wo_hbm, wo), (wu_hbm, wu), (wd_hbm, wd)))
    ]
    take_x = pltpu.make_async_copy(x_hbm, hb, o_sem.at[3])
    take_ct = pltpu.make_async_copy(ct_hbm, eb, o_sem.at[3])

    @pl.when(sec == 0)
    def _():
        take_x.start()

    @pl.when(sec == 1)
    def _():
        take_ct.start()

    for copy in weights:
        copy.start()

    barrier = pltpu.get_barrier_semaphore()
    peers = [s_to, y_to, (1 - sec, me, other)] + [x_to(bit) for bit in range(levels)]
    for peer in peers:
        pl.semaphore_signal(barrier, inc=1, device_id=peer, device_id_type=MESH)
    pl.semaphore_wait(barrier, len(peers))

    q_tiles, o_tiles, u_tiles = 3 * width // TILE, width // TILE, ff // TILE
    O_AT, U_AT, G_AT = q_tiles, tiles, tiles + u_tiles
    o_half, u_half = o_tiles // 2, u_tiles // 2
    UP, OUT, QKV = u_half, 2 * u_half, 2 * u_half + o_half
    A, DM, C, E = range(4)

    def own_tile(t):
        k = t - QKV
        at = jnp.where(t < OUT, U_AT + rep * u_half + t - UP, O_AT + rep * o_half + t - OUT)
        at = jnp.where(t < UP, G_AT + rep * u_half + t, at)
        return jnp.where(t < QKV, at, k // o_half * o_tiles + rep * o_half + k % o_half)

    def side_of(t):
        return jnp.where(t < UP, E, jnp.where(t < OUT, C, jnp.where(t < QKV, DM, A)))

    def remote(src, dst, ss, rs, to):
        return pltpu.make_async_remote_copy(
            src_ref=src, dst_ref=dst, send_sem=ss, recv_sem=rs, device_id=to, device_id_type=MESH
        )

    def forward_hop():
        return remote(out_ref, hb, p_send.at[0], p_recv.at[0], s_to)

    def backward_hop():
        return remote(dh_ref, eb, p_send.at[1], p_recv.at[1], s_to)

    def y_hop(n, src, dst):
        return remote(src, dst, y_send.at[n], y_recv.at[n], y_to)

    def y_act(n, src):
        return y_hop(n, src, pin.at[n])

    def cross_hop():
        return remote(dh_ref, pin.at[E], p_send.at[2], y_recv.at[E], (1 - sec, me, other))

    def y_mask():
        return y_hop(4, mask, mask2)

    def bit_of(level, t):
        return jnp.where(t % 3 == 2, 1 - level, level) if level < 2 else level

    def half_of(level, t):
        return me // (1 << bit_of(level, t)) % 2 if level >= 2 else jnp.where(bit_of(level, t) == 0, me % 2, me // 2 % 2)

    def peer_of(level, t):
        stride = jnp.where(bit_of(level, t) == 0, 1, 2) if level < 2 else 1 << level
        return (sec, me + stride - 2 * stride * half_of(level, t), rep)

    def x_tile(level, t):
        return remote(
            sends[level].at[t, 1 - half_of(level, t)] if level else sends[0].at[t],
            arrivals[level].at[t], x_send.at[level, t], x_recv.at[level, t], peer_of(level, t),
        )

    def g_tile(t):
        return remote(ag.at[rep, t], ag.at[rep, t], g_send.at[t], g_recv.at[t], y_to)

    def small_hop(n):
        to = x_to(levels - n) if n else y_to
        return remote(small.at[2 * n], small.at[2 * n + 1], s_send.at[n], s_recv.at[n], to)

    def transpose_into(lt, m, ref):
        for b in range(width // 128):
            block = ref[:, b * 128 : (b + 1) * 128].T
            size = min(shard, 128)
            for q in range(128 // size):
                first = b * 128 + q * size
                j = first // shard
                lt[m, j % 2, j // 2, first % shard : first % shard + size, :] = block[q * size : (q + 1) * size]

    row_at = lax.broadcasted_iota(jnp.int32, (BLOCK, BLOCK), 0)
    col_at = lax.broadcasted_iota(jnp.int32, (BLOCK, BLOCK), 1)
    base = (row_at // SEG == col_at // SEG) & (col_at <= row_at)
    per = BLOCK // SEG
    for b in range(blocks):
        first = jnp.zeros((BLOCK, BLOCK), jnp.int32)
        for j in range(per):
            first = jnp.where(col_at // SEG == j, SEG - count_ref[b * per + j], first)
        allowed = base & ((col_at % SEG >= first) | (col_at == row_at))
        mask[b] = jnp.where(allowed, 1.0, 0.0)
    acc[...] = jnp.zeros_like(acc)

    LN = 128

    def row_loop(body):
        def run(i, carry):
            body(pl.ds(pl.multiple_of(i * LN, LN), LN))
            return carry

        lax.fori_loop(0, rows // LN, run, 0)

    def tile_loop(count, body):
        def run(t, carry):
            body(t, pl.ds(pl.multiple_of(t * TILE, TILE), TILE))
            return carry

        lax.fori_loop(0, count, run, 0)

    y_mask().start()

    def share_grad():
        y_act(E, eb).start()
        transpose_into(lt, E, eb)

    @pl.when(sec == 0)
    def _():
        take_x.wait()

    @pl.when(sec == 1)
    def _():
        take_ct.wait()
        share_grad()
        forward_hop().wait_recv()

    def first_norm(at):
        normed, inverse = normalize(hb[at].astype(f32))
        norm1[at] = normed
        inv1[at] = inverse
        ab[at] = (normed * gain_ref[0, 0:1] + bias_ref[0, 0:1]).astype(bf16)

    row_loop(first_norm)

    y_act(A, ab).start()
    weights[0].wait()

    def cols_of(t):
        return pl.ds(pl.multiple_of(t * TILE, TILE), TILE)

    def project(t, at):
        pb[:, at] = mul(ab[...], wq[:, at]).astype(bf16)

    tile_loop(q_tiles, project)

    def pairs_of(first, count):
        return [(b, first + u, u) for u in range(count) for b in range(blocks)]

    def part(b, member, h):
        return pb[b * BLOCK : (b + 1) * BLOCK, pl.ds(pl.multiple_of(member * width + h * HEAD, HEAD), HEAD)]

    def tile_at(first, b, h):
        group = TILE // HEAD
        cols = pl.ds(pl.multiple_of((h % group) * HEAD, HEAD), HEAD)
        return (first + h // group, pl.ds(b * BLOCK, BLOCK), cols)

    def chances_of(pairs, mask):
        scores = [mul(part(b, 0, h), part(b, 1, h), NT) for b, h, _ in pairs]
        chances = []
        for (b, h, _), score in zip(pairs, scores):
            score = jnp.where(mask[b] > 0.5, score * scale, -1e30)
            raised = jnp.exp(score - jnp.max(score, axis=-1, keepdims=True))
            chance = raised * (1.0 / jnp.sum(raised, axis=-1, keepdims=True))
            probs[b, h] = chance
            chances.append(chance.astype(bf16))
        return chances

    def attend(pairs, mask, store, first):
        for (b, h, u), chance in zip(pairs, chances_of(pairs, mask)):
            store[tile_at(first, b, u)] = mul(chance, part(b, 2, h)).astype(bf16)

    attend(pairs_of(0, heads), mask, ra, O_AT)
    weights[1].wait()

    def attention_out(t, at):
        total = hb[:, at].astype(f32)
        for k in range(o_tiles):
            total = total + mul(ra[O_AT + k], wo[k * TILE : (k + 1) * TILE, at])
        mm[:, at] = total

    tile_loop(o_tiles, attention_out)

    def second_norm(at):
        normed, inverse = normalize(mm[at])
        norm2[at] = normed
        inv2[at] = inverse
        cb[at] = (normed * gain_ref[0, 1:2] + bias_ref[0, 1:2]).astype(bf16)

    row_loop(second_norm)

    y_act(C, cb).start()
    weights[2].wait()

    def feed_up(t, at, source, store, first):
        value, slope = gelu_pair(mul(source[...], wu[:, at]))
        store[first + t] = value.astype(bf16)
        gp[:, at] = slope

    tile_loop(u_tiles, partial(feed_up, source=cb, store=ra, first=G_AT))
    weights[3].wait()

    def feed_down(t, at):
        total = mm[:, at]
        for k in range(u_tiles):
            total = total + mul(ra[G_AT + k], wd[k * TILE : (k + 1) * TILE, at])
        out_ref[:, at] = total.astype(bf16)

    tile_loop(o_tiles, feed_down)

    @pl.when(sec == 0)
    def _():
        forward_hop().start()

    out_copy = pltpu.make_async_copy(out_ref, out_hbm, o_sem.at[0])
    out_copy.start()

    transpose_into(lt, C, cb)
    transpose_into(lt, A, ab)

    def meet_c():
        y_act(C, cb).wait_recv()
        transpose_into(ltr, C, pin.at[C])

    def meet_a():
        y_act(A, ab).wait_recv()
        transpose_into(ltr, A, pin.at[A])

    @pl.when(sec == 0)
    def _():
        meet_c()
        meet_a()
        backward_hop().wait_recv()
        transpose_into(lt, E, eb)

    def piece(v, j, t):
        alt = t % 3 == 2
        return jnp.where(alt, j % 2, v), jnp.where(alt, j // 2 * 2 + v, j)

    def product(t, v):
        tile = t // per_tile
        cols = pl.ds(pl.multiple_of(t % per_tile * CUT, CUT), CUT)
        h, r = side_of(tile), own_tile(tile)
        places = [piece(v, j, t) for j in range(dp // 2)]
        mine = jnp.concatenate([lt[h, a, b] for a, b in places], axis=0)
        theirs = jnp.concatenate([ltr[h, a, b] for a, b in places], axis=0)
        return mul(mine, ra[r, :, cols]) + mul(theirs, rr[tile, :, cols])

    def open_tile(t):
        part_sum = product(t, 1 - half_of(0, t)).astype(bf16)
        for j in range(dp // 2):
            sends[0][t, j] = part_sum[j * shard : (j + 1) * shard]
        x_tile(0, t).start()

    def open_range(first, last):
        def run(t, carry):
            open_tile(t)
            return carry

        lax.fori_loop(first, last, run, 0)

    def merge(level, t):
        count = dp >> (level + 1)
        if level == 0:
            part_sum = product(t, half_of(0, t))
            x_tile(0, t).wait_recv()
            kept = [part_sum[j * shard : (j + 1) * shard] for j in range(count)]
        else:
            x_tile(level, t).wait_recv()
            kept = [sends[level][t, half_of(level, t), j].astype(f32) for j in range(count)]
        for j in range(count):
            total = (kept[j] + arrivals[level][t, j].astype(f32)).astype(bf16)
            if level + 1 < levels:
                sends[level + 1][t, j % 2, j // 2] = total
            else:
                ag[rep, t] = total
        if level + 1 < levels:
            x_tile(level + 1, t).start()
        else:
            g_tile(t).start()

    def merge_range(first, last):
        def run(t, carry):
            merge(0, t)
            return carry

        lax.fori_loop(first, last, run, 0)

    def on(section, run):
        pl.when(sec == section)(run)

    def feed_down_back(t, at, source, store, first):
        store[first + t] = (mul(source[...], wd[at, :], NT) * gp[:, at]).astype(bf16)

    tile_loop(u_tiles, partial(feed_down_back, source=eb, store=ra, first=U_AT))

    def half_up(t, _):
        feed_up(t, cols_of(rep * u_half + t), pin.at[C], rr, 0)
        open_range(t * per_tile, (t + 1) * per_tile)

    def half_down_back(t, _):
        feed_down_back(t, cols_of(rep * u_half + t), pin.at[E], rr, UP)
        open_range((UP + t) * per_tile, (UP + t + 1) * per_tile)

    def feed_half():
        on(1, meet_c)
        y_act(E, eb).wait_recv()
        transpose_into(ltr, E, pin.at[E])
        tile_loop(u_half, half_up)

    def feed_up_back(t, at):
        total = mul(ra[U_AT], wu[at, 0:TILE], NT)
        for k in range(1, u_tiles):
            total = total + mul(ra[U_AT + k], wu[at, k * TILE : (k + 1) * TILE], NT)
        dcb[:, at] = total

    tile_loop(o_tiles, feed_up_back)

    def add_rows(i, value):
        acc[i] += jnp.sum(value.reshape(LN // 8, 8, width), axis=0)

    def second_back(at):
        d_c, normed = dcb[at], norm2[at]
        add_rows(1, d_c * normed)
        add_rows(3, d_c)
        d_m = eb[at].astype(f32) + normalize_back(d_c * gain_ref[0, 1:2], normed, inv2[at])
        mm[at] = d_m
        dmb[at] = d_m.astype(bf16)

    row_loop(second_back)

    y_act(DM, dmb).start()
    on(1, feed_half)

    def attention_out_back(t, at, source):
        dob[:, at] = mul(source[...], wo[at, :], NT).astype(bf16)

    tile_loop(o_tiles, partial(attention_out_back, source=dmb))

    transpose_into(lt, DM, dmb)

    def attend_back(pairs, store, first, stride):
        def d_out(b, h):
            return dob[b * BLOCK : (b + 1) * BLOCK, pl.ds(pl.multiple_of(h * HEAD, HEAD), HEAD)]

        d_chances = [mul(d_out(b, h), part(b, 2, h), NT) for b, h, _ in pairs]
        for b, h, u in pairs:
            d_v = mul(probs[b, h].astype(bf16), d_out(b, h), TN)
            store[tile_at(first + 2 * stride, b, u)] = d_v.astype(bf16)
        d_scores = []
        for (b, h, _), d_probs in zip(pairs, d_chances):
            chance = probs[b, h]
            inner = jnp.sum(chance * d_probs, axis=-1, keepdims=True)
            d_scores.append((chance * (d_probs - inner)).astype(bf16))
        for (b, h, u), d_s in zip(pairs, d_scores):
            store[tile_at(first, b, u)] = (mul(d_s, part(b, 1, h)) * scale).astype(bf16)
        for (b, h, u), d_s in zip(pairs, d_scores):
            store[tile_at(first + stride, b, u)] = (mul(d_s, part(b, 0, h), TN) * scale).astype(bf16)

    attend_back(pairs_of(0, heads), ra, 0, o_tiles)

    def project_back(t, at):
        total = mul(ra[0], wq[at, 0:TILE], NT)
        for k in range(1, q_tiles):
            total = total + mul(ra[k], wq[at, k * TILE : (k + 1) * TILE], NT)
        dcb[:, at] = total

    def first_back(at):
        d_a, normed = dcb[at], norm1[at]
        add_rows(0, d_a * normed)
        add_rows(2, d_a)
        d_h = mm[at] + normalize_back(d_a * gain_ref[0, 0:1], normed, inv1[at])
        dh_ref[at] = d_h.astype(bf16)

    dh_copy = pltpu.make_async_copy(dh_ref, dh_hbm, o_sem.at[1])

    def input_back():
        tile_loop(o_tiles, project_back)
        row_loop(first_back)
        dh_copy.start()

    @pl.when(sec == 1)
    def _():
        input_back()
        backward_hop().start()
        cross_hop().start()
        meet_a()

    @pl.when(sec == 0)
    def _():
        input_back()
        feed_half()

    tile_loop(u_half, half_down_back)
    merge_range(0, 4)

    def half_project(t, _):
        at = cols_of(t // o_half * o_tiles + rep * o_half + t % o_half)
        pb[:, at] = mul(pin[A], wq[:, at]).astype(bf16)

    tile_loop(3 * o_half, half_project)
    y_mask().wait_recv()
    half = pairs_of(rep * (heads // 2), heads // 2)
    attend(half, mask2, rr, OUT)
    y_act(DM, dmb).wait_recv()
    transpose_into(ltr, DM, pin.at[DM])
    open_range(OUT * per_tile, QKV * per_tile)
    merge_range(4, 6)

    def half_out_back(t, _):
        attention_out_back(t, cols_of(rep * o_half + t), pin.at[DM])

    tile_loop(o_half, half_out_back)
    attend_back(half, rr, QKV, o_half)

    for i in range(4):
        small[0, i : i + 1] = jnp.sum(acc[i], axis=0, keepdims=True)
        small[0, 4 + i : 5 + i] = jnp.zeros((1, width), f32)
    small_hop(0).start()

    def small_merge(n):
        small_hop(n).wait_recv()
        small[2 * n + 2] = small[2 * n] + small[2 * n + 1]
        if n < levels:
            small_hop(n + 1).start()

    lags = [3 * level - 3 for level in range(levels)]
    opened = QKV * per_tile

    def reduce_step(s, carry):
        @pl.when(s + opened < cuts)
        def _():
            open_tile(s + opened)

        @pl.when(s + 6 < cuts)
        def _():
            merge(0, s + 6)

        for level, lag in enumerate(lags[1:], 1):

            @pl.when((s >= lag) & (s < cuts + lag))
            def _():
                merge(level, s - lag)

        for n in range(levels + 1):

            @pl.when(s == 4 * n + 3)
            def _():
                small_merge(n)

        return carry

    lax.fori_loop(0, cuts + lags[-1], reduce_step, 0)

    if shard % 128 == 0:
        small_ref[...] = small[2 * levels + 2, :, pl.ds(pl.multiple_of(me * shard, shard), shard)]
    else:
        small_ref[...] = small[2 * levels + 2]

    def drain(t, carry):
        g_tile(t).wait_recv()
        for level in range(levels):
            x_tile(level, t).wait_send()
        g_tile(t).wait_send()
        return carry

    lax.fori_loop(0, cuts, drain, 0)
    grads_copy = pltpu.make_async_copy(ag, grad_hbm, o_sem.at[2])
    grads_copy.start()
    y_mask().wait_send()
    for n in (A, DM, C):
        y_act(n, ab).wait_send()

    for n in range(levels + 1):
        small_hop(n).wait_send()

    @pl.when(sec == 0)
    def _():
        forward_hop().wait_send()

    @pl.when(sec == 1)
    def _():
        backward_hop().wait_send()
        cross_hop().wait_send()
        y_act(E, eb).wait_send()

    out_copy.wait()
    dh_copy.wait()
    grads_copy.wait()


def finish_kernel(
    turn, grad_hbm, out_hbm, dh_hbm, small_ref, gq_hbm, go_hbm, gu_hbm, gd_hbm, out_to, dh_to, gain_ref, bias_ref,
    raw, kept, q, o, u, d, in_sem, out_sem,
):
    cuts, width, ff = raw.shape[1], kept.shape[2], u.shape[1]
    gain_ref[0] = small_ref[0:2]
    bias_ref[0] = small_ref[2:4]
    quarter = ff // 2 // CUT
    sizes = (quarter, quarter, width // 2 // CUT, 3 * width // 2 // CUT)
    copies = [(out_hbm, out_to), (dh_hbm, dh_to)]
    loads = []
    for n, (source, _) in enumerate(copies):
        loads.append(pltpu.make_async_copy(source, kept.at[n], in_sem.at[n]))
    for r in range(2):
        first = 0
        for size in sizes:
            at = pl.ds(first, size)
            loads.append(pltpu.make_async_copy(grad_hbm.at[r, at], raw.at[r, at], in_sem.at[len(loads)]))
            first += size
    for load in loads:
        load.start()
    stores = []

    def store(source, target):
        stores.append(pltpu.make_async_copy(source, target, out_sem.at[len(stores)]))
        stores[-1].start()

    def place(buffer, target, turned, r, first, count, at):
        for c in range(count):
            piece = raw[r, first + c]
            cols = slice(at + c * CUT, at + (c + 1) * CUT)
            if turned and turn:
                buffer[cols, :] = piece.astype(f32).T
            else:
                buffer[:, cols] = piece.astype(f32)
        size = count * CUT
        if turned and turn:
            store(buffer.at[pl.ds(at, size)], target.at[0, pl.ds(at, size)])
        else:
            store(buffer.at[:, pl.ds(at, size)], target.at[0, :, pl.ds(at, size)])

    for n, (_, target) in enumerate(copies):
        loads[n].wait()
        store(kept.at[n], target.at[0])
    n = 2
    for r in range(2):
        first = 0
        for size, (buffer, target, turned) in zip(sizes, ((d, gd_hbm, True), (u, gu_hbm, False), (o, go_hbm, True), (q, gq_hbm, False))):
            loads[n].wait()
            n += 1
            if buffer is q:
                for m in range(3):
                    place(buffer, target, turned, r, first + m * (size // 3), size // 3, m * width + r * (width // 2))
            else:
                place(buffer, target, turned, r, first, size, r * size * CUT)
            first += size
    for copy in stores:
        copy.wait()


def per_device(inputs, cotangent, seg_counts, w_qkv, w_out, w_up, w_down, gains, biases):
    dp = lax.axis_size("dp")
    levels = dp.bit_length() - 1
    rows, width = inputs.shape
    ff = w_up.shape[2]
    shard = width // dp
    whole_lanes = shard % 128 == 0
    tiles = 2 * ff // TILE
    cuts = tiles * TILE // CUT
    q_tiles, o_tiles, u_tiles = 3 * width // TILE, width // TILE, ff // TILE
    blocks, heads = rows // BLOCK, width // HEAD
    dma = pltpu.SemaphoreType.DMA
    vm = pltpu.VMEM
    act = vm((rows, width), bf16)
    wide = vm((rows, width), f32)
    scratch = [
        vm((width, 3 * width), bf16), vm((width, width), bf16), vm((width, ff), bf16), vm((ff, width), bf16),
        act, act, wide, wide, vm((rows, 1), f32), vm((rows, 1), f32),
        act, vm((rows, 3 * width), bf16), act, act, act,
        vm((blocks, heads, BLOCK, BLOCK), f32), wide, vm((rows, ff), f32), wide,
        vm((4, 8, width), f32), vm((blocks, BLOCK, BLOCK), f32),
        vm((blocks, BLOCK, BLOCK), f32), vm((4, rows, width), bf16),
        act, act,
        vm((4, 2, dp // 2, shard, rows), bf16),
        vm((4, 2, dp // 2, shard, rows), bf16),
        vm((2 * tiles, rows, TILE), bf16),
        vm((tiles, rows, TILE), bf16),
        vm((2, cuts, shard, CUT), bf16),
        vm((2 * levels + 3, 8, width), f32),
        vm((cuts, dp // 2, shard, CUT), bf16),
        *[vm((cuts, 2, dp >> (level + 1), shard, CUT), bf16) for level in range(1, levels)],
        *[vm((cuts, dp >> (level + 1), shard, CUT), bf16) for level in range(levels)],
        dma((4,)), dma((4,)),
        dma((5,)), dma((5,)),
        dma((levels, cuts)), dma((levels, cuts)),
        dma((cuts,)), dma((cuts,)),
        dma((levels + 1,)), dma((levels + 1,)),
        dma((3,)), dma((2,)),
    ]
    vspec = pl.BlockSpec(memory_space=pltpu.VMEM)
    hbm = pl.BlockSpec(memory_space=pl.ANY)
    sds = jax.ShapeDtypeStruct
    out, d_h, grads, small = pl.pallas_call(
        step_kernel,
        out_shape=(
            sds((rows, width), bf16), sds((rows, width), bf16),
            sds((2, cuts, shard, CUT), bf16),
            sds((8, shard if whole_lanes else width), f32),
        ),
        in_specs=[hbm, hbm, pl.BlockSpec(memory_space=pltpu.SMEM)] + [hbm] * 4 + [vspec] * 2,
        out_specs=(hbm, hbm, hbm, vspec),
        scratch_shapes=scratch,
        name="layers_step",
        compiler_params=pltpu.CompilerParams(
            collective_id=0, has_side_effects=True, vmem_limit_bytes=67043328
        ),
    )(inputs, cotangent, seg_counts, w_qkv, w_out, w_up, w_down, gains, biases)

    def shaped(n, turn):
        return (n, shard) if turn and whole_lanes else (shard, n)

    if not whole_lanes:
        small = lax.dynamic_slice_in_dim(small, lax.axis_index("dp") * shard, shard, 1)
    ends = ((3 * width, False), (width, True), (ff, False), (ff, True))
    g_q, g_o, g_u, g_d, out, d_h, gain_grads, bias_grads = pl.pallas_call(
        partial(finish_kernel, whole_lanes),
        out_shape=[sds((1, *shaped(n, turn)), f32) for n, turn in ends]
        + [sds((1, rows, width), bf16)] * 2
        + [sds((1, 2, shard), f32)] * 2,
        in_specs=[hbm, hbm, hbm, vspec],
        out_specs=[hbm] * 6 + [vspec] * 2,
        scratch_shapes=[
            vm((2, cuts, shard, CUT), bf16), vm((2, rows, width), bf16),
            *[vm(shaped(n, turn), f32) for n, turn in ends],
            dma((10,)), dma((16,)),
        ],
        name="finish",
    )(grads, out, d_h, small)
    if not whole_lanes:
        g_o, g_d = jnp.swapaxes(g_o, 1, 2), jnp.swapaxes(g_d, 1, 2)
    return (out, d_h, g_q, g_o, g_u, g_d, gain_grads, bias_grads)


def solution(mesh):
    rows = P(("dp", "rep"), None)
    layer = P("section", None, None)
    return jax.shard_map(
        per_device,
        mesh=mesh,
        in_specs=(rows, rows, P(("dp", "rep"))) + (layer,) * 6,
        out_specs=(
            P("section", ("dp", "rep"), None),
            P("section", ("dp", "rep"), None),
            P("section", "dp", None),
            P("section", None, "dp"),
            P("section", "dp", None),
            P("section", None, "dp"),
            P("section", None, "dp"),
            P("section", None, "dp"),
        ),
        check_vma=False,
    )
```

```python
from functools import partial

import jax
import jax.numpy as jnp
from jax import lax
from jax.experimental import pallas as pl
from jax.experimental.pallas import tpu as pltpu
from jax.sharding import PartitionSpec as P

SEG = 16
HEAD = 128
BLOCK = 128
TILE = 512
CUT = 256
MESH = pl.DeviceIdType.MESH
epsilon = 1e-05
f32 = jnp.float32
bf16 = jnp.bfloat16
NN = (((1,), (0,)), ((), ()))
NT = (((1,), (1,)), ((), ()))
TN = (((0,), (0,)), ((), ()))


def mul(left, right, dims=NN):
    return lax.dot_general(left, right, dims, preferred_element_type=f32)


def normalize(hidden):
    average = jnp.mean(hidden, axis=-1, keepdims=True)
    centred = hidden - average
    inverse = lax.rsqrt(jnp.mean(centred * centred, axis=-1, keepdims=True) + epsilon)
    return (centred * inverse, inverse)


def normalize_back(grad_normed, normed, inverse):
    centre_term = jnp.mean(grad_normed, axis=-1, keepdims=True)
    slope_term = normed * jnp.mean(grad_normed * normed, axis=-1, keepdims=True)
    return inverse * (grad_normed - centre_term - slope_term)


def gelu_pair(u):
    k = 0.7978845608
    square = u * u
    t = jnp.tanh(k * (u + 0.044715 * u * square))
    half = 0.5 * (1.0 + t)
    slope = half + 0.5 * u * (1.0 - t * t) * (k * (1.0 + 3 * 0.044715 * square))
    return u * half, slope


def step_kernel(
    x_hbm, ct_hbm, count_ref, wq_hbm, wo_hbm, wu_hbm, wd_hbm, gain_ref, bias_ref,
    out_hbm, dh_hbm, grad_hbm, small_ref,
    wq, wo, wu, wd, hb, eb, norm1, norm2, inv1, inv2, ab, pb, cb, dmb, dob, probs, mm, gp, dcb, acc, mask,
    mask2, pin, out_ref, dh_ref, lt, ltr, ra, rr, ag, small, *rest,
):
    dp = lt.shape[1] * lt.shape[2]
    levels = dp.bit_length() - 1
    sends, arrivals = rest[:levels], rest[levels : 2 * levels]
    w_sem, o_sem, y_send, y_recv, x_send, x_recv, g_send, g_recv, s_send, s_recv, p_send, p_recv = rest[2 * levels :]
    rows, width = hb.shape
    blocks = rows // BLOCK
    heads = width // HEAD
    ff = wu.shape[1]
    shard = width // dp
    tiles = ra.shape[0] // 2
    cuts = ag.shape[1]
    per_tile = cuts // tiles
    scale = HEAD**-0.5
    sec = lax.axis_index("section")
    me = lax.axis_index("dp")
    rep = lax.axis_index("rep")
    other = 1 - rep
    y_to = (sec, me, other)
    s_to = (1 - sec, me, rep)

    def x_to(bit):
        stride = 1 << bit
        return (sec, me + stride - 2 * stride * (me // stride % 2), rep)

    weights = [
        pltpu.make_async_copy(src.at[0], dst, w_sem.at[i])
        for i, (src, dst) in enumerate(((wo_hbm, wo), (wu_hbm, wu), (wd_hbm, wd)))
    ]
    members = []
    for i in range(3):
        at = pl.ds(i * width, width)
        members.append(pltpu.make_async_copy(wq_hbm.at[0, :, at], wq.at[:, at], w_sem.at[3 + i]))
    take_x = pltpu.make_async_copy(x_hbm, hb, o_sem.at[3])
    take_ct = pltpu.make_async_copy(ct_hbm, eb, o_sem.at[3])

    @pl.when(sec == 0)
    def _():
        take_x.start()

    @pl.when(sec == 1)
    def _():
        take_ct.start()

    for copy in members:
        copy.start()

    barrier = pltpu.get_barrier_semaphore()
    peers = [s_to, y_to, (1 - sec, me, other)] + [x_to(bit) for bit in range(levels)]
    for peer in peers:
        pl.semaphore_signal(barrier, inc=1, device_id=peer, device_id_type=MESH)
    pl.semaphore_wait(barrier, len(peers))

    q_tiles, o_tiles, u_tiles = 3 * width // TILE, width // TILE, ff // TILE
    O_AT, U_AT, G_AT = q_tiles, tiles, tiles + u_tiles
    o_half, u_half = o_tiles // 2, u_tiles // 2
    UP, OUT, QKV = u_half, 2 * u_half, 2 * u_half + o_half
    A, DM, C, E = range(4)

    def own_tile(t):
        k = t - QKV
        at = jnp.where(t < OUT, U_AT + rep * u_half + t - UP, O_AT + rep * o_half + t - OUT)
        at = jnp.where(t < UP, G_AT + rep * u_half + t, at)
        return jnp.where(t < QKV, at, k // o_half * o_tiles + rep * o_half + k % o_half)

    def side_of(t):
        return jnp.where(t < UP, E, jnp.where(t < OUT, C, jnp.where(t < QKV, DM, A)))

    def remote(src, dst, ss, rs, to):
        return pltpu.make_async_remote_copy(
            src_ref=src, dst_ref=dst, send_sem=ss, recv_sem=rs, device_id=to, device_id_type=MESH
        )

    def forward_hop():
        return remote(out_ref, hb, p_send.at[0], p_recv.at[0], s_to)

    def backward_hop():
        return remote(dh_ref, eb, p_send.at[1], p_recv.at[1], s_to)

    def y_hop(n, src, dst):
        return remote(src, dst, y_send.at[n], y_recv.at[n], y_to)

    def y_act(n, src):
        return y_hop(n, src, pin.at[n])

    def cross_hop():
        return remote(dh_ref, pin.at[E], p_send.at[2], y_recv.at[E], (1 - sec, me, other))

    def y_mask():
        return y_hop(4, mask, mask2)

    def bit_of(level, t):
        return jnp.where(t % 3 == 1, 1 - level, level) if level < 2 else level

    def half_of(level, t):
        return me // (1 << bit_of(level, t)) % 2 if level >= 2 else jnp.where(bit_of(level, t) == 0, me % 2, me // 2 % 2)

    def peer_of(level, t):
        stride = jnp.where(bit_of(level, t) == 0, 1, 2) if level < 2 else 1 << level
        return (sec, me + stride - 2 * stride * half_of(level, t), rep)

    def x_tile(level, t):
        return remote(
            sends[level].at[t, 1 - half_of(level, t)] if level else sends[0].at[t],
            arrivals[level].at[t], x_send.at[level, t], x_recv.at[level, t], peer_of(level, t),
        )

    def g_tile(t):
        return remote(ag.at[rep, t], ag.at[rep, t], g_send.at[t], g_recv.at[t], y_to)

    def small_hop(n):
        to = x_to(levels - n) if n else y_to
        return remote(small.at[2 * n], small.at[2 * n + 1], s_send.at[n], s_recv.at[n], to)

    def transpose_into(lt, m, ref):
        for b in range(width // 128):
            block = ref[:, b * 128 : (b + 1) * 128].T
            size = min(shard, 128)
            for q in range(128 // size):
                first = b * 128 + q * size
                j = first // shard
                lt[m, j % 2, j // 2, first % shard : first % shard + size, :] = block[q * size : (q + 1) * size]

    row_at = lax.broadcasted_iota(jnp.int32, (BLOCK, BLOCK), 0)
    col_at = lax.broadcasted_iota(jnp.int32, (BLOCK, BLOCK), 1)
    base = (row_at // SEG == col_at // SEG) & (col_at <= row_at)
    per = BLOCK // SEG
    for b in range(blocks):
        first = jnp.zeros((BLOCK, BLOCK), jnp.int32)
        for j in range(per):
            first = jnp.where(col_at // SEG == j, SEG - count_ref[b * per + j], first)
        allowed = base & ((col_at % SEG >= first) | (col_at == row_at))
        mask[b] = jnp.where(allowed, 1.0, 0.0)
    acc[...] = jnp.zeros_like(acc)

    LN = 128

    def row_loop(body):
        def run(i, carry):
            body(pl.ds(pl.multiple_of(i * LN, LN), LN))
            return carry

        lax.fori_loop(0, rows // LN, run, 0)

    def tile_loop(count, body):
        def run(t, carry):
            body(t, pl.ds(pl.multiple_of(t * TILE, TILE), TILE))
            return carry

        lax.fori_loop(0, count, run, 0)

    y_mask().start()

    def share_grad():
        y_act(E, eb).start()
        transpose_into(lt, E, eb)

    @pl.when(sec == 0)
    def _():
        take_x.wait()

    @pl.when(sec == 1)
    def _():
        take_ct.wait()
        share_grad()
        forward_hop().wait_recv()

    def first_norm(at):
        normed, inverse = normalize(hb[at].astype(f32))
        norm1[at] = normed
        inv1[at] = inverse
        ab[at] = (normed * gain_ref[0, 0:1] + bias_ref[0, 0:1]).astype(bf16)

    row_loop(first_norm)

    y_act(A, ab).start()
    def cols_of(t):
        return pl.ds(pl.multiple_of(t * TILE, TILE), TILE)

    def project(t, at):
        pb[:, at] = mul(ab[...], wq[:, at]).astype(bf16)

    for i, copy in enumerate(members):
        copy.wait()

        if i == 1:
            for rest_copy in weights:
                rest_copy.start()

        def project_member(t, _):
            project(t, cols_of(i * o_tiles + t))

        tile_loop(o_tiles, project_member)


    def pairs_of(first, count):
        return [(b, first + u, u) for u in range(count) for b in range(blocks)]

    def part(b, member, h):
        return pb[b * BLOCK : (b + 1) * BLOCK, pl.ds(pl.multiple_of(member * width + h * HEAD, HEAD), HEAD)]

    def tile_at(first, b, h):
        group = TILE // HEAD
        cols = pl.ds(pl.multiple_of((h % group) * HEAD, HEAD), HEAD)
        return (first + h // group, pl.ds(b * BLOCK, BLOCK), cols)

    def chances_of(pairs, mask):
        scores = [mul(part(b, 0, h), part(b, 1, h), NT) for b, h, _ in pairs]
        chances = []
        for (b, h, _), score in zip(pairs, scores):
            score = jnp.where(mask[b] > 0.5, score * scale, -1e30)
            raised = jnp.exp(score - jnp.max(score, axis=-1, keepdims=True))
            chance = raised * (1.0 / jnp.sum(raised, axis=-1, keepdims=True))
            probs[b, h] = chance
            chances.append(chance.astype(bf16))
        return chances

    def attend(pairs, mask, store, first):
        for (b, h, u), chance in zip(pairs, chances_of(pairs, mask)):
            store[tile_at(first, b, u)] = mul(chance, part(b, 2, h)).astype(bf16)

    attend(pairs_of(0, heads), mask, ra, O_AT)
    weights[0].wait()

    def attention_out(t, at):
        total = hb[:, at].astype(f32)
        for k in range(o_tiles):
            total = total + mul(ra[O_AT + k], wo[k * TILE : (k + 1) * TILE, at])
        mm[:, at] = total

    tile_loop(o_tiles, attention_out)

    def second_norm(at):
        normed, inverse = normalize(mm[at])
        norm2[at] = normed
        inv2[at] = inverse
        cb[at] = (normed * gain_ref[0, 1:2] + bias_ref[0, 1:2]).astype(bf16)

    row_loop(second_norm)

    y_act(C, cb).start()
    weights[1].wait()

    def feed_up(t, at, source, store, first):
        value, slope = gelu_pair(mul(source[...], wu[:, at]))
        store[first + t] = value.astype(bf16)
        gp[:, at] = slope

    tile_loop(u_tiles, partial(feed_up, source=cb, store=ra, first=G_AT))
    weights[2].wait()

    def feed_down(t, at):
        total = mm[:, at]
        for k in range(u_tiles):
            total = total + mul(ra[G_AT + k], wd[k * TILE : (k + 1) * TILE, at])
        out_ref[:, at] = total.astype(bf16)

    tile_loop(o_tiles, feed_down)

    @pl.when(sec == 0)
    def _():
        forward_hop().start()

    out_copy = pltpu.make_async_copy(out_ref, out_hbm, o_sem.at[0])
    out_copy.start()

    transpose_into(lt, C, cb)
    transpose_into(lt, A, ab)

    def meet_c():
        y_act(C, cb).wait_recv()
        transpose_into(ltr, C, pin.at[C])

    def meet_a():
        y_act(A, ab).wait_recv()
        transpose_into(ltr, A, pin.at[A])

    @pl.when(sec == 0)
    def _():
        meet_c()
        meet_a()
        backward_hop().wait_recv()
        transpose_into(lt, E, eb)

    def piece(v, j, t):
        alt = t % 3 == 1
        return jnp.where(alt, j % 2, v), jnp.where(alt, j // 2 * 2 + v, j)

    def product(t, v):
        tile = t // per_tile
        cols = pl.ds(pl.multiple_of(t % per_tile * CUT, CUT), CUT)
        h, r = side_of(tile), own_tile(tile)
        places = [piece(v, j, t) for j in range(dp // 2)]
        mine = jnp.concatenate([lt[h, a, b] for a, b in places], axis=0)
        theirs = jnp.concatenate([ltr[h, a, b] for a, b in places], axis=0)
        return mul(mine, ra[r, :, cols]) + mul(theirs, rr[tile, :, cols])

    def open_tile(t):
        part_sum = product(t, 1 - half_of(0, t)).astype(bf16)
        for j in range(dp // 2):
            sends[0][t, j] = part_sum[j * shard : (j + 1) * shard]
        x_tile(0, t).start()

    def open_range(first, last):
        def run(t, carry):
            open_tile(t)
            return carry

        lax.fori_loop(first, last, run, 0)

    def merge(level, t):
        count = dp >> (level + 1)
        if level == 0:
            part_sum = product(t, half_of(0, t))
            x_tile(0, t).wait_recv()
            kept = [part_sum[j * shard : (j + 1) * shard] for j in range(count)]
        else:
            x_tile(level, t).wait_recv()
            kept = [sends[level][t, half_of(level, t), j].astype(f32) for j in range(count)]
        for j in range(count):
            total = (kept[j] + arrivals[level][t, j].astype(f32)).astype(bf16)
            if level + 1 < levels:
                sends[level + 1][t, j % 2, j // 2] = total
            else:
                ag[rep, t] = total
        if level + 1 < levels:
            x_tile(level + 1, t).start()
        else:
            g_tile(t).start()

    def merge_range(first, last):
        def run(t, carry):
            merge(0, t)
            return carry

        lax.fori_loop(first, last, run, 0)

    def on(section, run):
        pl.when(sec == section)(run)

    def feed_down_back(t, at, source, store, first):
        store[first + t] = (mul(source[...], wd[at, :], NT) * gp[:, at]).astype(bf16)

    tile_loop(u_tiles, partial(feed_down_back, source=eb, store=ra, first=U_AT))

    def half_up(t, _):
        feed_up(t, cols_of(rep * u_half + t), pin.at[C], rr, 0)
        open_range(t * per_tile, (t + 1) * per_tile)

    def half_down_back(t, _):
        feed_down_back(t, cols_of(rep * u_half + t), pin.at[E], rr, UP)
        open_range((UP + t) * per_tile, (UP + t + 1) * per_tile)

    def feed_half():
        on(1, meet_c)
        y_act(E, eb).wait_recv()
        transpose_into(ltr, E, pin.at[E])
        tile_loop(u_half, half_up)

    def feed_up_back(t, at):
        total = mul(ra[U_AT], wu[at, 0:TILE], NT)
        for k in range(1, u_tiles):
            total = total + mul(ra[U_AT + k], wu[at, k * TILE : (k + 1) * TILE], NT)
        dcb[:, at] = total

    tile_loop(o_tiles, feed_up_back)

    def add_rows(i, value):
        acc[i] += jnp.sum(value.reshape(LN // 8, 8, width), axis=0)

    def second_back(at):
        d_c, normed = dcb[at], norm2[at]
        add_rows(1, d_c * normed)
        add_rows(3, d_c)
        d_m = eb[at].astype(f32) + normalize_back(d_c * gain_ref[0, 1:2], normed, inv2[at])
        mm[at] = d_m
        dmb[at] = d_m.astype(bf16)

    row_loop(second_back)

    y_act(DM, dmb).start()
    on(1, feed_half)

    def attention_out_back(t, at, source):
        dob[:, at] = mul(source[...], wo[at, :], NT).astype(bf16)

    tile_loop(o_tiles, partial(attention_out_back, source=dmb))

    transpose_into(lt, DM, dmb)

    def attend_back(pairs, store, first, stride):
        def d_out(b, h):
            return dob[b * BLOCK : (b + 1) * BLOCK, pl.ds(pl.multiple_of(h * HEAD, HEAD), HEAD)]

        d_chances = [mul(d_out(b, h), part(b, 2, h), NT) for b, h, _ in pairs]
        for b, h, u in pairs:
            d_v = mul(probs[b, h].astype(bf16), d_out(b, h), TN)
            store[tile_at(first + 2 * stride, b, u)] = d_v.astype(bf16)
        d_scores = []
        for (b, h, _), d_probs in zip(pairs, d_chances):
            chance = probs[b, h]
            inner = jnp.sum(chance * d_probs, axis=-1, keepdims=True)
            d_scores.append((chance * (d_probs - inner)).astype(bf16))
        for (b, h, u), d_s in zip(pairs, d_scores):
            store[tile_at(first, b, u)] = (mul(d_s, part(b, 1, h)) * scale).astype(bf16)
        for (b, h, u), d_s in zip(pairs, d_scores):
            store[tile_at(first + stride, b, u)] = (mul(d_s, part(b, 0, h), TN) * scale).astype(bf16)

    attend_back(pairs_of(0, heads), ra, 0, o_tiles)

    def project_back(t, at):
        total = mul(ra[0], wq[at, 0:TILE], NT)
        for k in range(1, q_tiles):
            total = total + mul(ra[k], wq[at, k * TILE : (k + 1) * TILE], NT)
        dcb[:, at] = total

    def first_back(at):
        d_a, normed = dcb[at], norm1[at]
        add_rows(0, d_a * normed)
        add_rows(2, d_a)
        d_h = mm[at] + normalize_back(d_a * gain_ref[0, 0:1], normed, inv1[at])
        dh_ref[at] = d_h.astype(bf16)

    dh_copy = pltpu.make_async_copy(dh_ref, dh_hbm, o_sem.at[1])

    def input_back():
        tile_loop(o_tiles, project_back)
        row_loop(first_back)
        dh_copy.start()

    @pl.when(sec == 1)
    def _():
        input_back()
        backward_hop().start()
        cross_hop().start()
        meet_a()

    @pl.when(sec == 0)
    def _():
        input_back()
        feed_half()

    tile_loop(u_half, half_down_back)
    merge_range(0, 2)

    def half_project(t, _):
        at = cols_of(t // o_half * o_tiles + rep * o_half + t % o_half)
        pb[:, at] = mul(pin[A], wq[:, at]).astype(bf16)

    tile_loop(3 * o_half, half_project)
    y_mask().wait_recv()
    half = pairs_of(rep * (heads // 2), heads // 2)
    attend(half, mask2, rr, OUT)
    y_act(DM, dmb).wait_recv()
    transpose_into(ltr, DM, pin.at[DM])
    open_range(OUT * per_tile, QKV * per_tile)
    merge_range(2, 3)

    def half_out_back(t, _):
        attention_out_back(t, cols_of(rep * o_half + t), pin.at[DM])

    tile_loop(o_half, half_out_back)
    attend_back(half, rr, QKV, o_half)

    for i in range(4):
        small[0, i : i + 1] = jnp.sum(acc[i], axis=0, keepdims=True)
        small[0, 4 + i : 5 + i] = jnp.zeros((1, width), f32)
    small_hop(0).start()

    def small_merge(n):
        small_hop(n).wait_recv()
        small[2 * n + 2] = small[2 * n] + small[2 * n + 1]
        if n < levels:
            small_hop(n + 1).start()

    lags = [3 * level - 3 for level in range(levels)]
    opened = QKV * per_tile

    def reduce_step(s, carry):
        @pl.when(s + opened < cuts)
        def _():
            open_tile(s + opened)

        for level, lag in reversed(list(enumerate(lags[1:], 1))):

            @pl.when((s >= lag) & (s < cuts + lag))
            def _():
                merge(level, s - lag)

        @pl.when(s + 3 < cuts)
        def _():
            merge(0, s + 3)

        for n in range(levels + 1):

            @pl.when(s == 4 * n + 3)
            def _():
                small_merge(n)

        return carry

    lax.fori_loop(0, cuts + lags[-1], reduce_step, 0)

    if shard % 128 == 0:
        small_ref[...] = small[2 * levels + 2, :, pl.ds(pl.multiple_of(me * shard, shard), shard)]
    else:
        small_ref[...] = small[2 * levels + 2]

    def take_cut(t):
        return pltpu.make_async_copy(ag.at[:, t], grad_hbm.at[:, t], o_sem.at[4 + t])

    def finish_cut(t, carry):
        g_tile(t).wait_recv()
        take_cut(t).start()
        return carry

    lax.fori_loop(0, cuts, finish_cut, 0)

    def drain(t, carry):
        take_cut(t).wait()
        for level in range(levels):
            x_tile(level, t).wait_send()
        g_tile(t).wait_send()
        return carry

    lax.fori_loop(0, cuts, drain, 0)
    y_mask().wait_send()
    for n in (A, DM, C):
        y_act(n, ab).wait_send()

    for n in range(levels + 1):
        small_hop(n).wait_send()

    @pl.when(sec == 0)
    def _():
        forward_hop().wait_send()

    @pl.when(sec == 1)
    def _():
        backward_hop().wait_send()
        cross_hop().wait_send()
        y_act(E, eb).wait_send()

    out_copy.wait()
    dh_copy.wait()


def finish_kernel(
    turn, grad_hbm, out_hbm, dh_hbm, small_ref, gq_hbm, go_hbm, gu_hbm, gd_hbm, out_to, dh_to, gain_ref, bias_ref,
    raw, kept, q, o, u, d, in_sem, out_sem,
):
    cuts, width, ff = raw.shape[1], kept.shape[2], u.shape[1]
    gain_ref[0] = small_ref[0:2]
    bias_ref[0] = small_ref[2:4]
    quarter = ff // 2 // CUT
    sizes = (quarter, quarter, width // 2 // CUT, 3 * width // 2 // CUT)
    copies = [(out_hbm, out_to), (dh_hbm, dh_to)]
    loads = []
    for n, (source, _) in enumerate(copies):
        loads.append(pltpu.make_async_copy(source, kept.at[n], in_sem.at[n]))
    for r in range(2):
        first = 0
        for size in sizes:
            at = pl.ds(first, size)
            loads.append(pltpu.make_async_copy(grad_hbm.at[r, at], raw.at[r, at], in_sem.at[len(loads)]))
            first += size
    for load in loads:
        load.start()
    stores = []

    def store(source, target):
        stores.append(pltpu.make_async_copy(source, target, out_sem.at[len(stores)]))
        stores[-1].start()

    def place(buffer, target, turned, r, first, count, at):
        for c in range(count):
            piece = raw[r, first + c]
            cols = slice(at + c * CUT, at + (c + 1) * CUT)
            if turned and turn:
                buffer[cols, :] = piece.T.astype(f32)
            else:
                buffer[:, cols] = piece.astype(f32)
        size = count * CUT
        if turned and turn:
            store(buffer.at[pl.ds(at, size)], target.at[0, pl.ds(at, size)])
        else:
            store(buffer.at[:, pl.ds(at, size)], target.at[0, :, pl.ds(at, size)])

    for n, (_, target) in enumerate(copies):
        loads[n].wait()
        store(kept.at[n], target.at[0])
    n = 2
    for r in range(2):
        first = 0
        for size, (buffer, target, turned) in zip(sizes, ((d, gd_hbm, True), (u, gu_hbm, False), (o, go_hbm, True), (q, gq_hbm, False))):
            loads[n].wait()
            n += 1
            if buffer is q:
                for m in range(3):
                    place(buffer, target, turned, r, first + m * (size // 3), size // 3, m * width + r * (width // 2))
            else:
                place(buffer, target, turned, r, first, size, r * size * CUT)
            first += size
    for copy in stores:
        copy.wait()


def per_device(inputs, cotangent, seg_counts, w_qkv, w_out, w_up, w_down, gains, biases):
    dp = lax.axis_size("dp")
    levels = dp.bit_length() - 1
    rows, width = inputs.shape
    ff = w_up.shape[2]
    shard = width // dp
    whole_lanes = shard % 128 == 0
    tiles = 2 * ff // TILE
    cuts = tiles * TILE // CUT
    q_tiles, o_tiles, u_tiles = 3 * width // TILE, width // TILE, ff // TILE
    blocks, heads = rows // BLOCK, width // HEAD
    dma = pltpu.SemaphoreType.DMA
    vm = pltpu.VMEM
    act = vm((rows, width), bf16)
    wide = vm((rows, width), f32)
    scratch = [
        vm((width, 3 * width), bf16), vm((width, width), bf16), vm((width, ff), bf16), vm((ff, width), bf16),
        act, act, wide, wide, vm((rows, 1), f32), vm((rows, 1), f32),
        act, vm((rows, 3 * width), bf16), act, act, act,
        vm((blocks, heads, BLOCK, BLOCK), f32), wide, vm((rows, ff), f32), wide,
        vm((4, 8, width), f32), vm((blocks, BLOCK, BLOCK), f32),
        vm((blocks, BLOCK, BLOCK), f32), vm((4, rows, width), bf16),
        act, act,
        vm((4, 2, dp // 2, shard, rows), bf16),
        vm((4, 2, dp // 2, shard, rows), bf16),
        vm((2 * tiles, rows, TILE), bf16),
        vm((tiles, rows, TILE), bf16),
        vm((2, cuts, shard, CUT), bf16),
        vm((2 * levels + 3, 8, width), f32),
        vm((cuts, dp // 2, shard, CUT), bf16),
        *[vm((cuts, 2, dp >> (level + 1), shard, CUT), bf16) for level in range(1, levels)],
        *[vm((cuts, dp >> (level + 1), shard, CUT), bf16) for level in range(levels)],
        dma((6,)), dma((4 + cuts,)),
        dma((5,)), dma((5,)),
        dma((levels, cuts)), dma((levels, cuts)),
        dma((cuts,)), dma((cuts,)),
        dma((levels + 1,)), dma((levels + 1,)),
        dma((3,)), dma((2,)),
    ]
    vspec = pl.BlockSpec(memory_space=pltpu.VMEM)
    hbm = pl.BlockSpec(memory_space=pl.ANY)
    sds = jax.ShapeDtypeStruct
    out, d_h, grads, small = pl.pallas_call(
        step_kernel,
        out_shape=(
            sds((rows, width), bf16), sds((rows, width), bf16),
            sds((2, cuts, shard, CUT), bf16),
            sds((8, shard if whole_lanes else width), f32),
        ),
        in_specs=[hbm, hbm, pl.BlockSpec(memory_space=pltpu.SMEM)] + [hbm] * 4 + [vspec] * 2,
        out_specs=(hbm, hbm, hbm, vspec),
        scratch_shapes=scratch,
        name="layers_step",
        compiler_params=pltpu.CompilerParams(
            collective_id=0, has_side_effects=True, vmem_limit_bytes=67043328
        ),
    )(inputs, cotangent, seg_counts, w_qkv, w_out, w_up, w_down, gains, biases)

    def shaped(n, turn):
        return (n, shard) if turn and whole_lanes else (shard, n)

    if not whole_lanes:
        small = lax.dynamic_slice_in_dim(small, lax.axis_index("dp") * shard, shard, 1)
    ends = ((3 * width, False), (width, True), (ff, False), (ff, True))
    g_q, g_o, g_u, g_d, out, d_h, gain_grads, bias_grads = pl.pallas_call(
        partial(finish_kernel, whole_lanes),
        out_shape=[sds((1, *shaped(n, turn)), f32) for n, turn in ends]
        + [sds((1, rows, width), bf16)] * 2
        + [sds((1, 2, shard), f32)] * 2,
        in_specs=[hbm, hbm, hbm, vspec],
        out_specs=[hbm] * 6 + [vspec] * 2,
        scratch_shapes=[
            vm((2, cuts, shard, CUT), bf16), vm((2, rows, width), bf16),
            *[vm(shaped(n, turn), f32) for n, turn in ends],
            dma((10,)), dma((16,)),
        ],
        name="finish",
    )(grads, out, d_h, small)
    if not whole_lanes:
        g_o, g_d = jnp.swapaxes(g_o, 1, 2), jnp.swapaxes(g_d, 1, 2)
    return (out, d_h, g_q, g_o, g_u, g_d, gain_grads, bias_grads)


def solution(mesh):
    rows = P(("dp", "rep"), None)
    layer = P("section", None, None)
    return jax.shard_map(
        per_device,
        mesh=mesh,
        in_specs=(rows, rows, P(("dp", "rep"))) + (layer,) * 6,
        out_specs=(
            P("section", ("dp", "rep"), None),
            P("section", ("dp", "rep"), None),
            P("section", "dp", None),
            P("section", None, "dp"),
            P("section", "dp", None),
            P("section", None, "dp"),
            P("section", None, "dp"),
            P("section", None, "dp"),
        ),
        check_vma=False,
    )
```

```python
from functools import partial

import jax
import jax.numpy as jnp
from jax import lax
from jax.experimental import pallas as pl
from jax.experimental.pallas import tpu as pltpu
from jax.sharding import PartitionSpec as P

SEG = 16
HEAD = 128
BLOCK = 128
TILE = 512
CUT = 256
MESH = pl.DeviceIdType.MESH
epsilon = 1e-05
f32 = jnp.float32
bf16 = jnp.bfloat16
NN = (((1,), (0,)), ((), ()))
NT = (((1,), (1,)), ((), ()))
TN = (((0,), (0,)), ((), ()))


def mul(left, right, dims=NN):
    return lax.dot_general(left, right, dims, preferred_element_type=f32)


def normalize(hidden):
    average = jnp.mean(hidden, axis=-1, keepdims=True)
    centred = hidden - average
    inverse = lax.rsqrt(jnp.mean(centred * centred, axis=-1, keepdims=True) + epsilon)
    return (centred * inverse, inverse)


def normalize_back(grad_normed, normed, inverse):
    centre_term = jnp.mean(grad_normed, axis=-1, keepdims=True)
    slope_term = normed * jnp.mean(grad_normed * normed, axis=-1, keepdims=True)
    return inverse * (grad_normed - centre_term - slope_term)


def gelu_pair(u):
    k = 0.7978845608
    square = u * u
    t = jnp.tanh(k * (u + 0.044715 * u * square))
    half = 0.5 * (1.0 + t)
    slope = half + 0.5 * u * (1.0 - t * t) * (k * (1.0 + 3 * 0.044715 * square))
    return u * half, slope


def step_kernel(
    x_hbm, ct_hbm, count_ref, wq_hbm, wo_hbm, wu_hbm, wd_hbm, gain_ref, bias_ref,
    out_hbm, dh_hbm, grad_hbm, small_ref,
    wq, wo, wu, wd, hb, eb, norm1, norm2, inv1, inv2, ab, pb, cb, dmb, dob, probs, mm, gp, dcb, acc, mask,
    mask2, pin, out_ref, dh_ref, lt, ltr, ra, rr, ag, small, *rest,
):
    dp = lt.shape[1] * lt.shape[2]
    levels = dp.bit_length() - 1
    sends, arrivals = rest[:levels], rest[levels : 2 * levels]
    w_sem, o_sem, y_send, y_recv, x_send, x_recv, g_send, g_recv, s_send, s_recv, p_send, p_recv = rest[2 * levels :]
    rows, width = hb.shape
    blocks = rows // BLOCK
    heads = width // HEAD
    ff = wu.shape[1]
    shard = width // dp
    tiles = ra.shape[0] // 2
    cuts = ag.shape[1]
    per_tile = cuts // tiles
    scale = HEAD**-0.5
    sec = lax.axis_index("section")
    me = lax.axis_index("dp")
    rep = lax.axis_index("rep")
    other = 1 - rep
    y_to = (sec, me, other)
    s_to = (1 - sec, me, rep)

    def x_to(bit):
        stride = 1 << bit
        return (sec, me + stride - 2 * stride * (me // stride % 2), rep)

    weights = [
        pltpu.make_async_copy(src.at[0], dst, w_sem.at[i])
        for i, (src, dst) in enumerate(((wo_hbm, wo), (wu_hbm, wu), (wd_hbm, wd)))
    ]
    members = []
    for i in range(3):
        at = pl.ds(i * width, width)
        members.append(pltpu.make_async_copy(wq_hbm.at[0, :, at], wq.at[:, at], w_sem.at[3 + i]))
    take_x = pltpu.make_async_copy(x_hbm, hb, o_sem.at[3])
    take_ct = pltpu.make_async_copy(ct_hbm, eb, o_sem.at[3])

    @pl.when(sec == 0)
    def _():
        take_x.start()

    @pl.when(sec == 1)
    def _():
        take_ct.start()

    for copy in members:
        copy.start()

    barrier = pltpu.get_barrier_semaphore()
    peers = [s_to, y_to, (1 - sec, me, other)] + [x_to(bit) for bit in range(levels)]
    for peer in peers:
        pl.semaphore_signal(barrier, inc=1, device_id=peer, device_id_type=MESH)
    pl.semaphore_wait(barrier, len(peers))

    q_tiles, o_tiles, u_tiles = 3 * width // TILE, width // TILE, ff // TILE
    O_AT, U_AT, G_AT = q_tiles, tiles, tiles + u_tiles
    o_half, u_half = o_tiles // 2, u_tiles // 2
    UP, OUT, QKV = u_half, 2 * u_half, 2 * u_half + o_half
    A, DM, C, E = range(4)

    def own_tile(t):
        k = t - QKV
        at = jnp.where(t < OUT, U_AT + rep * u_half + t - UP, O_AT + rep * o_half + t - OUT)
        at = jnp.where(t < UP, G_AT + rep * u_half + t, at)
        return jnp.where(t < QKV, at, k // o_half * o_tiles + rep * o_half + k % o_half)

    def side_of(t):
        return jnp.where(t < UP, E, jnp.where(t < OUT, C, jnp.where(t < QKV, DM, A)))

    def remote(src, dst, ss, rs, to):
        return pltpu.make_async_remote_copy(
            src_ref=src, dst_ref=dst, send_sem=ss, recv_sem=rs, device_id=to, device_id_type=MESH
        )

    def forward_hop():
        return remote(out_ref, hb, p_send.at[0], p_recv.at[0], s_to)

    def backward_hop():
        return remote(dh_ref, eb, p_send.at[1], p_recv.at[1], s_to)

    def y_hop(n, src, dst):
        return remote(src, dst, y_send.at[n], y_recv.at[n], y_to)

    def y_act(n, src):
        return y_hop(n, src, pin.at[n])

    def cross_hop():
        return remote(dh_ref, pin.at[E], p_send.at[2], y_recv.at[E], (1 - sec, me, other))

    def y_mask():
        return y_hop(4, mask, mask2)

    def bit_of(level, t):
        return jnp.where(t % 3 == 1, 1 - level, level) if level < 2 else level

    def half_of(level, t):
        return me // (1 << bit_of(level, t)) % 2 if level >= 2 else jnp.where(bit_of(level, t) == 0, me % 2, me // 2 % 2)

    def peer_of(level, t):
        stride = jnp.where(bit_of(level, t) == 0, 1, 2) if level < 2 else 1 << level
        return (sec, me + stride - 2 * stride * half_of(level, t), rep)

    def x_tile(level, t):
        return remote(
            sends[level].at[t, 1 - half_of(level, t)] if level else sends[0].at[t],
            arrivals[level].at[t], x_send.at[level, t], x_recv.at[level, t], peer_of(level, t),
        )

    def g_tile(t):
        return remote(ag.at[rep, t], ag.at[rep, t], g_send.at[t], g_recv.at[t], y_to)

    def small_hop(n):
        to = x_to(levels - n) if n else y_to
        return remote(small.at[2 * n], small.at[2 * n + 1], s_send.at[n], s_recv.at[n], to)

    def transpose_into(lt, m, ref):
        for b in range(width // 128):
            block = ref[:, b * 128 : (b + 1) * 128].T
            size = min(shard, 128)
            for q in range(128 // size):
                first = b * 128 + q * size
                j = first // shard
                lt[m, j % 2, j // 2, first % shard : first % shard + size, :] = block[q * size : (q + 1) * size]

    row_at = lax.broadcasted_iota(jnp.int32, (BLOCK, BLOCK), 0)
    col_at = lax.broadcasted_iota(jnp.int32, (BLOCK, BLOCK), 1)
    base = (row_at // SEG == col_at // SEG) & (col_at <= row_at)
    per = BLOCK // SEG
    for b in range(blocks):
        first = jnp.zeros((BLOCK, BLOCK), jnp.int32)
        for j in range(per):
            first = jnp.where(col_at // SEG == j, SEG - count_ref[b * per + j], first)
        allowed = base & ((col_at % SEG >= first) | (col_at == row_at))
        mask[b] = jnp.where(allowed, 1.0, 0.0)
    acc[...] = jnp.zeros_like(acc)

    LN = 128

    def row_loop(body):
        def run(i, carry):
            body(pl.ds(pl.multiple_of(i * LN, LN), LN))
            return carry

        lax.fori_loop(0, rows // LN, run, 0)

    def tile_loop(count, body):
        def run(t, carry):
            body(t, pl.ds(pl.multiple_of(t * TILE, TILE), TILE))
            return carry

        lax.fori_loop(0, count, run, 0)

    y_mask().start()

    def share_grad():
        y_act(E, eb).start()
        transpose_into(lt, E, eb)

    @pl.when(sec == 0)
    def _():
        take_x.wait()

    @pl.when(sec == 1)
    def _():
        take_ct.wait()
        share_grad()
        forward_hop().wait_recv()

    def first_norm(at):
        normed, inverse = normalize(hb[at].astype(f32))
        norm1[at] = normed
        inv1[at] = inverse
        ab[at] = (normed * gain_ref[0, 0:1] + bias_ref[0, 0:1]).astype(bf16)

    row_loop(first_norm)

    y_act(A, ab).start()
    def cols_of(t):
        return pl.ds(pl.multiple_of(t * TILE, TILE), TILE)

    def project(t, at):
        pb[:, at] = mul(ab[...], wq[:, at]).astype(bf16)

    for i, copy in enumerate(members):
        copy.wait()

        if i == 1:
            for rest_copy in weights:
                rest_copy.start()

        def project_member(t, _):
            project(t, cols_of(i * o_tiles + t))

        tile_loop(o_tiles, project_member)


    def pairs_of(first, count):
        return [(b, first + u, u) for u in range(count) for b in range(blocks)]

    def part(b, member, h):
        return pb[b * BLOCK : (b + 1) * BLOCK, pl.ds(pl.multiple_of(member * width + h * HEAD, HEAD), HEAD)]

    def tile_at(first, b, h):
        group = TILE // HEAD
        cols = pl.ds(pl.multiple_of((h % group) * HEAD, HEAD), HEAD)
        return (first + h // group, pl.ds(b * BLOCK, BLOCK), cols)

    def chances_of(pairs, mask):
        scores = [mul(part(b, 0, h), part(b, 1, h), NT) for b, h, _ in pairs]
        chances = []
        for (b, h, _), score in zip(pairs, scores):
            score = jnp.where(mask[b] > 0.5, score * scale, -1e30)
            raised = jnp.exp(score - jnp.max(score, axis=-1, keepdims=True))
            chance = raised * (1.0 / jnp.sum(raised, axis=-1, keepdims=True))
            probs[b, h] = chance
            chances.append(chance.astype(bf16))
        return chances

    def attend(pairs, mask, store, first):
        for (b, h, u), chance in zip(pairs, chances_of(pairs, mask)):
            store[tile_at(first, b, u)] = mul(chance, part(b, 2, h)).astype(bf16)

    attend(pairs_of(0, heads), mask, ra, O_AT)
    weights[0].wait()

    def attention_out(t, at):
        total = hb[:, at].astype(f32)
        for k in range(o_tiles):
            total = total + mul(ra[O_AT + k], wo[k * TILE : (k + 1) * TILE, at])
        mm[:, at] = total

    tile_loop(o_tiles, attention_out)

    def second_norm(at):
        normed, inverse = normalize(mm[at])
        norm2[at] = normed
        inv2[at] = inverse
        cb[at] = (normed * gain_ref[0, 1:2] + bias_ref[0, 1:2]).astype(bf16)

    row_loop(second_norm)

    y_act(C, cb).start()
    weights[1].wait()

    def feed_up(t, at, source, store, first):
        value, slope = gelu_pair(mul(source[...], wu[:, at]))
        store[first + t] = value.astype(bf16)
        gp[:, at] = slope

    tile_loop(u_tiles, partial(feed_up, source=cb, store=ra, first=G_AT))
    weights[2].wait()

    def feed_down(t, at):
        total = mm[:, at]
        for k in range(u_tiles):
            total = total + mul(ra[G_AT + k], wd[k * TILE : (k + 1) * TILE, at])
        out_ref[:, at] = total.astype(bf16)

    tile_loop(o_tiles, feed_down)

    @pl.when(sec == 0)
    def _():
        forward_hop().start()

    out_copy = pltpu.make_async_copy(out_ref, out_hbm, o_sem.at[0])
    out_copy.start()

    transpose_into(lt, C, cb)
    transpose_into(lt, A, ab)

    def meet_c():
        y_act(C, cb).wait_recv()
        transpose_into(ltr, C, pin.at[C])

    def meet_a():
        y_act(A, ab).wait_recv()
        transpose_into(ltr, A, pin.at[A])

    @pl.when(sec == 0)
    def _():
        meet_c()
        meet_a()
        backward_hop().wait_recv()
        transpose_into(lt, E, eb)

    def piece(v, j, t):
        alt = t % 3 == 1
        return jnp.where(alt, j % 2, v), jnp.where(alt, j // 2 * 2 + v, j)

    def product(t, v):
        tile = t // per_tile
        cols = pl.ds(pl.multiple_of(t % per_tile * CUT, CUT), CUT)
        h, r = side_of(tile), own_tile(tile)
        places = [piece(v, j, t) for j in range(dp // 2)]
        mine = jnp.concatenate([lt[h, a, b] for a, b in places], axis=0)
        theirs = jnp.concatenate([ltr[h, a, b] for a, b in places], axis=0)
        return mul(mine, ra[r, :, cols]) + mul(theirs, rr[tile, :, cols])

    def open_tile(t):
        part_sum = product(t, 1 - half_of(0, t)).astype(bf16)
        for j in range(dp // 2):
            sends[0][t, j] = part_sum[j * shard : (j + 1) * shard]
        x_tile(0, t).start()

    def open_range(first, last):
        def run(t, carry):
            open_tile(t)
            return carry

        lax.fori_loop(first, last, run, 0)

    def merge(level, t):
        count = dp >> (level + 1)
        if level == 0:
            part_sum = product(t, half_of(0, t))
            x_tile(0, t).wait_recv()
            kept = [part_sum[j * shard : (j + 1) * shard] for j in range(count)]
        else:
            x_tile(level, t).wait_recv()
            kept = [sends[level][t, half_of(level, t), j].astype(f32) for j in range(count)]
        for j in range(count):
            total = (kept[j] + arrivals[level][t, j].astype(f32)).astype(bf16)
            if level + 1 < levels:
                sends[level + 1][t, j % 2, j // 2] = total
            else:
                ag[rep, t] = total
        if level + 1 < levels:
            x_tile(level + 1, t).start()
        else:
            g_tile(t).start()

    def merge_range(first, last):
        def run(t, carry):
            merge(0, t)
            return carry

        lax.fori_loop(first, last, run, 0)

    def on(section, run):
        pl.when(sec == section)(run)

    def feed_down_back(t, at, source, store, first):
        store[first + t] = (mul(source[...], wd[at, :], NT) * gp[:, at]).astype(bf16)

    tile_loop(u_tiles, partial(feed_down_back, source=eb, store=ra, first=U_AT))

    def half_up(t, _):
        feed_up(t, cols_of(rep * u_half + t), pin.at[C], rr, 0)
        open_range(t * per_tile, (t + 1) * per_tile)

    def half_down_back(t, _):
        feed_down_back(t, cols_of(rep * u_half + t), pin.at[E], rr, UP)
        open_range((UP + t) * per_tile, (UP + t + 1) * per_tile)

    def feed_half():
        on(1, meet_c)
        y_act(E, eb).wait_recv()
        transpose_into(ltr, E, pin.at[E])
        tile_loop(u_half, half_up)

    def feed_up_back(t, at):
        total = mul(ra[U_AT], wu[at, 0:TILE], NT)
        for k in range(1, u_tiles):
            total = total + mul(ra[U_AT + k], wu[at, k * TILE : (k + 1) * TILE], NT)
        dcb[:, at] = total

    tile_loop(o_tiles, feed_up_back)

    def add_rows(i, value):
        acc[i] += jnp.sum(value.reshape(LN // 8, 8, width), axis=0)

    def second_back(at):
        d_c, normed = dcb[at], norm2[at]
        add_rows(1, d_c * normed)
        add_rows(3, d_c)
        d_m = eb[at].astype(f32) + normalize_back(d_c * gain_ref[0, 1:2], normed, inv2[at])
        mm[at] = d_m
        dmb[at] = d_m.astype(bf16)

    row_loop(second_back)

    y_act(DM, dmb).start()
    on(1, feed_half)

    def attention_out_back(t, at, source):
        dob[:, at] = mul(source[...], wo[at, :], NT).astype(bf16)

    tile_loop(o_tiles, partial(attention_out_back, source=dmb))

    transpose_into(lt, DM, dmb)

    def attend_back(pairs, store, first, stride):
        def d_out(b, h):
            return dob[b * BLOCK : (b + 1) * BLOCK, pl.ds(pl.multiple_of(h * HEAD, HEAD), HEAD)]

        d_chances = [mul(d_out(b, h), part(b, 2, h), NT) for b, h, _ in pairs]
        for b, h, u in pairs:
            d_v = mul(probs[b, h].astype(bf16), d_out(b, h), TN)
            store[tile_at(first + 2 * stride, b, u)] = d_v.astype(bf16)
        d_scores = []
        for (b, h, _), d_probs in zip(pairs, d_chances):
            chance = probs[b, h]
            inner = jnp.sum(chance * d_probs, axis=-1, keepdims=True)
            d_scores.append((chance * (d_probs - inner)).astype(bf16))
        for (b, h, u), d_s in zip(pairs, d_scores):
            store[tile_at(first, b, u)] = (mul(d_s, part(b, 1, h)) * scale).astype(bf16)
        for (b, h, u), d_s in zip(pairs, d_scores):
            store[tile_at(first + stride, b, u)] = (mul(d_s, part(b, 0, h), TN) * scale).astype(bf16)

    attend_back(pairs_of(0, heads), ra, 0, o_tiles)

    def project_back(t, at):
        total = mul(ra[0], wq[at, 0:TILE], NT)
        for k in range(1, q_tiles):
            total = total + mul(ra[k], wq[at, k * TILE : (k + 1) * TILE], NT)
        dcb[:, at] = total

    def first_back(at):
        d_a, normed = dcb[at], norm1[at]
        add_rows(0, d_a * normed)
        add_rows(2, d_a)
        d_h = mm[at] + normalize_back(d_a * gain_ref[0, 0:1], normed, inv1[at])
        dh_ref[at] = d_h.astype(bf16)

    dh_copy = pltpu.make_async_copy(dh_ref, dh_hbm, o_sem.at[1])

    def input_back():
        tile_loop(o_tiles, project_back)
        row_loop(first_back)
        dh_copy.start()

    @pl.when(sec == 1)
    def _():
        input_back()
        backward_hop().start()
        cross_hop().start()
        meet_a()

    @pl.when(sec == 0)
    def _():
        input_back()
        feed_half()

    tile_loop(u_half, half_down_back)
    merge_range(0, 3)

    def half_project(t, _):
        at = cols_of(t // o_half * o_tiles + rep * o_half + t % o_half)
        pb[:, at] = mul(pin[A], wq[:, at]).astype(bf16)

    tile_loop(3 * o_half, half_project)
    y_mask().wait_recv()
    half = pairs_of(rep * (heads // 2), heads // 2)
    attend(half, mask2, rr, OUT)
    y_act(DM, dmb).wait_recv()
    transpose_into(ltr, DM, pin.at[DM])
    open_range(OUT * per_tile, QKV * per_tile)
    merge_range(3, 4)

    def half_out_back(t, _):
        attention_out_back(t, cols_of(rep * o_half + t), pin.at[DM])

    tile_loop(o_half, half_out_back)
    attend_back(half, rr, QKV, o_half)

    for i in range(4):
        small[0, i : i + 1] = jnp.sum(acc[i], axis=0, keepdims=True)
        small[0, 4 + i : 5 + i] = jnp.zeros((1, width), f32)
    small_hop(0).start()

    def small_merge(n):
        small_hop(n).wait_recv()
        small[2 * n + 2] = small[2 * n] + small[2 * n + 1]
        if n < levels:
            small_hop(n + 1).start()

    lags = [3 * level - 3 for level in range(levels)]
    opened = QKV * per_tile

    def reduce_step(s, carry):
        @pl.when(s + opened < cuts)
        def _():
            open_tile(s + opened)

        for level, lag in reversed(list(enumerate(lags[1:], 1))):

            @pl.when((s >= lag) & (s < cuts + lag))
            def _():
                merge(level, s - lag)

        @pl.when(s + 4 < cuts)
        def _():
            merge(0, s + 4)

        for n in range(levels + 1):

            @pl.when(s == 4 * n + 3)
            def _():
                small_merge(n)

        return carry

    lax.fori_loop(0, cuts + lags[-1], reduce_step, 0)

    if shard % 128 == 0:
        small_ref[...] = small[2 * levels + 2, :, pl.ds(pl.multiple_of(me * shard, shard), shard)]
    else:
        small_ref[...] = small[2 * levels + 2]

    def take_cut(t):
        return pltpu.make_async_copy(ag.at[:, t], grad_hbm.at[:, t], o_sem.at[4 + t])

    def finish_cut(t, carry):
        g_tile(t).wait_recv()
        take_cut(t).start()
        return carry

    lax.fori_loop(0, cuts, finish_cut, 0)

    def drain(t, carry):
        take_cut(t).wait()
        for level in range(levels):
            x_tile(level, t).wait_send()
        g_tile(t).wait_send()
        return carry

    lax.fori_loop(0, cuts, drain, 0)
    y_mask().wait_send()
    for n in (A, DM, C):
        y_act(n, ab).wait_send()

    for n in range(levels + 1):
        small_hop(n).wait_send()

    @pl.when(sec == 0)
    def _():
        forward_hop().wait_send()

    @pl.when(sec == 1)
    def _():
        backward_hop().wait_send()
        cross_hop().wait_send()
        y_act(E, eb).wait_send()

    out_copy.wait()
    dh_copy.wait()


def finish_kernel(
    turn, grad_hbm, out_hbm, dh_hbm, small_ref, gq_hbm, go_hbm, gu_hbm, gd_hbm, out_to, dh_to, gain_ref, bias_ref,
    raw, kept, q, o, u, d, in_sem, out_sem,
):
    cuts, width, ff = raw.shape[1], kept.shape[2], u.shape[1]
    gain_ref[0] = small_ref[0:2]
    bias_ref[0] = small_ref[2:4]
    quarter = ff // 2 // CUT
    sizes = (quarter, quarter, width // 2 // CUT, 3 * width // 2 // CUT)
    copies = [(out_hbm, out_to), (dh_hbm, dh_to)]
    loads = []
    for n, (source, _) in enumerate(copies):
        loads.append(pltpu.make_async_copy(source, kept.at[n], in_sem.at[n]))
    for r in range(2):
        first = 0
        for size in sizes:
            at = pl.ds(first, size)
            loads.append(pltpu.make_async_copy(grad_hbm.at[r, at], raw.at[r, at], in_sem.at[len(loads)]))
            first += size
    for load in loads:
        load.start()
    stores = []

    def store(source, target):
        stores.append(pltpu.make_async_copy(source, target, out_sem.at[len(stores)]))
        stores[-1].start()

    def place(buffer, target, turned, r, first, count, at):
        for c in range(count):
            piece = raw[r, first + c]
            cols = slice(at + c * CUT, at + (c + 1) * CUT)
            if turned and turn:
                buffer[cols, :] = piece.T.astype(f32)
            else:
                buffer[:, cols] = piece.astype(f32)
        size = count * CUT
        if turned and turn:
            store(buffer.at[pl.ds(at, size)], target.at[0, pl.ds(at, size)])
        else:
            store(buffer.at[:, pl.ds(at, size)], target.at[0, :, pl.ds(at, size)])

    for n, (_, target) in enumerate(copies):
        loads[n].wait()
        store(kept.at[n], target.at[0])
    n = 2
    for r in range(2):
        first = 0
        for size, (buffer, target, turned) in zip(sizes, ((d, gd_hbm, True), (u, gu_hbm, False), (o, go_hbm, True), (q, gq_hbm, False))):
            loads[n].wait()
            n += 1
            if buffer is q:
                for m in range(3):
                    place(buffer, target, turned, r, first + m * (size // 3), size // 3, m * width + r * (width // 2))
            else:
                place(buffer, target, turned, r, first, size, r * size * CUT)
            first += size
    for copy in stores:
        copy.wait()


def per_device(inputs, cotangent, seg_counts, w_qkv, w_out, w_up, w_down, gains, biases):
    dp = lax.axis_size("dp")
    levels = dp.bit_length() - 1
    rows, width = inputs.shape
    ff = w_up.shape[2]
    shard = width // dp
    whole_lanes = shard % 128 == 0
    tiles = 2 * ff // TILE
    cuts = tiles * TILE // CUT
    q_tiles, o_tiles, u_tiles = 3 * width // TILE, width // TILE, ff // TILE
    blocks, heads = rows // BLOCK, width // HEAD
    dma = pltpu.SemaphoreType.DMA
    vm = pltpu.VMEM
    act = vm((rows, width), bf16)
    wide = vm((rows, width), f32)
    scratch = [
        vm((width, 3 * width), bf16), vm((width, width), bf16), vm((width, ff), bf16), vm((ff, width), bf16),
        act, act, wide, wide, vm((rows, 1), f32), vm((rows, 1), f32),
        act, vm((rows, 3 * width), bf16), act, act, act,
        vm((blocks, heads, BLOCK, BLOCK), f32), wide, vm((rows, ff), f32), wide,
        vm((4, 8, width), f32), vm((blocks, BLOCK, BLOCK), f32),
        vm((blocks, BLOCK, BLOCK), f32), vm((4, rows, width), bf16),
        act, act,
        vm((4, 2, dp // 2, shard, rows), bf16),
        vm((4, 2, dp // 2, shard, rows), bf16),
        vm((2 * tiles, rows, TILE), bf16),
        vm((tiles, rows, TILE), bf16),
        vm((2, cuts, shard, CUT), bf16),
        vm((2 * levels + 3, 8, width), f32),
        vm((cuts, dp // 2, shard, CUT), bf16),
        *[vm((cuts, 2, dp >> (level + 1), shard, CUT), bf16) for level in range(1, levels)],
        *[vm((cuts, dp >> (level + 1), shard, CUT), bf16) for level in range(levels)],
        dma((6,)), dma((4 + cuts,)),
        dma((5,)), dma((5,)),
        dma((levels, cuts)), dma((levels, cuts)),
        dma((cuts,)), dma((cuts,)),
        dma((levels + 1,)), dma((levels + 1,)),
        dma((3,)), dma((2,)),
    ]
    vspec = pl.BlockSpec(memory_space=pltpu.VMEM)
    hbm = pl.BlockSpec(memory_space=pl.ANY)
    sds = jax.ShapeDtypeStruct
    out, d_h, grads, small = pl.pallas_call(
        step_kernel,
        out_shape=(
            sds((rows, width), bf16), sds((rows, width), bf16),
            sds((2, cuts, shard, CUT), bf16),
            sds((8, shard if whole_lanes else width), f32),
        ),
        in_specs=[hbm, hbm, pl.BlockSpec(memory_space=pltpu.SMEM)] + [hbm] * 4 + [vspec] * 2,
        out_specs=(hbm, hbm, hbm, vspec),
        scratch_shapes=scratch,
        name="layers_step",
        compiler_params=pltpu.CompilerParams(
            collective_id=0, has_side_effects=True, vmem_limit_bytes=67043328
        ),
    )(inputs, cotangent, seg_counts, w_qkv, w_out, w_up, w_down, gains, biases)

    def shaped(n, turn):
        return (n, shard) if turn and whole_lanes else (shard, n)

    if not whole_lanes:
        small = lax.dynamic_slice_in_dim(small, lax.axis_index("dp") * shard, shard, 1)
    ends = ((3 * width, False), (width, True), (ff, False), (ff, True))
    g_q, g_o, g_u, g_d, out, d_h, gain_grads, bias_grads = pl.pallas_call(
        partial(finish_kernel, whole_lanes),
        out_shape=[sds((1, *shaped(n, turn)), f32) for n, turn in ends]
        + [sds((1, rows, width), bf16)] * 2
        + [sds((1, 2, shard), f32)] * 2,
        in_specs=[hbm, hbm, hbm, vspec],
        out_specs=[hbm] * 6 + [vspec] * 2,
        scratch_shapes=[
            vm((2, cuts, shard, CUT), bf16), vm((2, rows, width), bf16),
            *[vm(shaped(n, turn), f32) for n, turn in ends],
            dma((10,)), dma((16,)),
        ],
        name="finish",
    )(grads, out, d_h, small)
    if not whole_lanes:
        g_o, g_d = jnp.swapaxes(g_o, 1, 2), jnp.swapaxes(g_d, 1, 2)
    return (out, d_h, g_q, g_o, g_u, g_d, gain_grads, bias_grads)


def solution(mesh):
    rows = P(("dp", "rep"), None)
    layer = P("section", None, None)
    return jax.shard_map(
        per_device,
        mesh=mesh,
        in_specs=(rows, rows, P(("dp", "rep"))) + (layer,) * 6,
        out_specs=(
            P("section", ("dp", "rep"), None),
            P("section", ("dp", "rep"), None),
            P("section", "dp", None),
            P("section", None, "dp"),
            P("section", "dp", None),
            P("section", None, "dp"),
            P("section", None, "dp"),
            P("section", None, "dp"),
        ),
        check_vma=False,
    )
```
